32 devices in a mesh: dp: 8 (over z, x), cent: 4 (over y, core).
Axes of the slice: x: 2, y: 2, z: 4, core: 2. Of those that a mesh axis runs over, the one named last changes fastest.
Arguments:
- embeddings: bfloat16 [8192, 512], P('dp'), may hold values from -60 to 60, as said below
- centroids: bfloat16 [16384, 512], P('cent'), may hold values from -60 to 60, as said below
Outputs:
- new_centroids: float32 [16384, 512], P(('cent', 'dp'))
- column_mass: float32 [16384], P(('cent', 'dp'))
The draws below stay inside these ranges and needn't reach their ends.
Inputs may be any that keep to these rules, and one draw needn't show every extreme that they name: `embeddings`: every row is nonzero. `centroids`: every row is nonzero.
All inputs are finite; a program needn't handle non-finite values.
Results may differ from the reference program's by a relative error of at most 0.00074.
Values sent between devices are 32-bit elements; how exact they have to be, the bound alone decides.
A program may use at most 128 MiB of HBM per device.

```python
import math
import jax
import jax.numpy as jnp
from jax import lax

D = 512
K = 16384
ROWS_DEV = 1024
ITERS = 3
ROWS = 8192
N_DP = 8


def cluster_directions(key, width):
    common = jax.random.fold_in(key, 5)
    return jnp.clip(jax.random.normal(common, (8, width), jnp.float32), -4.0, 4.0)


def cluster_members(key, salt, count):
    first, second = jax.random.split(jax.random.fold_in(key, salt))
    cluster_order = jax.random.permutation(first, 8)
    ticket = jax.random.randint(second, (count,), 0, 36)
    bucket_edges = jnp.array([1, 3, 6, 10, 15, 21, 28], jnp.int32)
    bucket = jnp.sum((ticket[:, None] >= bucket_edges[None, :]).astype(jnp.int32), axis=1)
    return jnp.take(cluster_order, bucket, axis=0)


def scaled_rows(key, salt, count, width):
    directions = cluster_directions(key, width)
    members = cluster_members(key, salt + 1, count)
    first, second, third = jax.random.split(jax.random.fold_in(key, salt), 3)
    row_scale = jnp.exp(jax.random.uniform(second, (count, 1), jnp.float32, 0.0, math.log(10.0)))
    strength = jax.random.uniform(third, (count, 1), jnp.float32, 0.5, 1.0)
    noise_part = jnp.clip(jax.random.normal(first, (count, width), jnp.float32), -5.0, 5.0)
    picked = jnp.take(directions, members, axis=0)
    return jnp.clip(noise_part + strength * picked, -6.0, 6.0) * row_scale


def draw_embeddings(key, part):
    return scaled_rows(key, 11, ROWS, D).astype(jnp.bfloat16)


def draw_centroids(key, part):
    return scaled_rows(key, 23, K, D).astype(jnp.bfloat16)


def setup_inputs(seed: int = 0) -> dict:
    arg_keys = jax.random.split(jax.random.key(seed), 3)
    return {
        "embeddings": draw_embeddings(jax.random.fold_in(arg_keys[2], 71), 0),
        "centroids": draw_centroids(jax.random.fold_in(arg_keys[2], 71), 0),
    }


TAU = 0.02

def rms_rows(values):
    wide = values.astype(jnp.float32)
    return (wide * lax.rsqrt(lax.optimization_barrier(jnp.mean(wide * wide, axis=1, keepdims=True)) + 1e-06)).astype(jnp.bfloat16)

def energy_block(rows_block, cent_rows):
    scores = lax.dot_general(rows_block, cent_rows, (((1,), (1,)), ((), ())), preferred_element_type=jnp.float32)
    return jnp.exp(scores * (1.0 / (TAU * D)))

def reference(embeddings, centroids):
    high = lax.Precision.HIGHEST
    xh = rms_rows(embeddings)
    ch = rms_rows(centroids)
    blocks = xh.reshape(N_DP, ROWS_DEV, D)
    ratio = float(ROWS) / float(K)

    def sums(u, v):

        def step(carry, item):
            block, weights = item
            energy = energy_block(block, ch)
            rows_sum = jnp.dot(energy, v, precision=high)
            return (carry + jnp.dot(weights, energy, precision=high), rows_sum)
        cols, rows_sum = lax.scan(step, jnp.zeros((K,), jnp.float32), (blocks, u.reshape(N_DP, ROWS_DEV)))
        return (rows_sum.reshape(ROWS), cols)
    u = jnp.ones((ROWS,), jnp.float32)
    v = jnp.ones((K,), jnp.float32)
    for step_index in range(ITERS):
        rows_sum, cols = sums(u, v)
        u, v = (jnp.sqrt(u / rows_sum), jnp.sqrt(v * ratio / cols))

    def final_step(carry, item):
        cols, weighted = carry
        block, weights = item
        energy = energy_block(block, ch)
        cols = cols + jnp.dot(weights, energy, precision=high)
        plan = (float(K) * weights[:, None] * energy * v[None, :]).astype(jnp.bfloat16)
        weighted = weighted + lax.dot_general(plan, block, (((0,), (0,)), ((), ())), preferred_element_type=jnp.float32)
        return ((cols, weighted), None)
    init = (jnp.zeros((K,), jnp.float32), jnp.zeros((K, D), jnp.float32))
    (cols, weighted), unused = lax.scan(final_step, init, (blocks, u.reshape(N_DP, ROWS_DEV)))
    column_mass = v * cols * (float(K) / float(ROWS))
    new_centroids = weighted * lax.rsqrt(lax.optimization_barrier(jnp.mean(weighted * weighted, axis=1, keepdims=True)) + 1e-06)
    return (new_centroids, column_mass)
```

```python
import functools
import jax
import jax.numpy as jnp
from jax import lax
from jax.experimental import pallas as pl
from jax.experimental.pallas import tpu as pltpu
from jax.sharding import PartitionSpec as P

ITERS = 3
TAU = 0.02
MESH = pl.DeviceIdType.MESH
NT = (((1,), (1,)), ((), ()))
NB = 8
CHUNK = 256
PIECES = 4
PLAN = {
    "start": (0, 1),
    "scores": {2: (2,), 5: (3,)},
    "exchange0": (4,),
    "pass1": {1: (5,)},
    "exchange1": (6,),
    "pass2": {1: (7,)},
    "exchange2": (8,),
    "u": (9,),
    "weigh": {3: (10,), 6: (11,)},
    "end": (12, 13, 14),
}


def rms_rows(values):
    wide = values.astype(jnp.float32)
    return (wide * lax.rsqrt(jnp.mean(wide * wide, axis=1, keepdims=True) + 1e-06)).astype(
        jnp.bfloat16
    )


def lane_tiles(values):
    total = values[:, :128]
    for t in range(1, values.shape[1] // 128):
        total = total + values[:, t * 128 : (t + 1) * 128]
    return total


def to_column(row):
    return jnp.broadcast_to(row, (128, row.shape[1])).T


def to_row(tile):
    return jnp.sum(tile.T, axis=0, keepdims=True)


def kernel(
    total_rows, total_cents, n_dp, n_cent,
    emb_hbm, cent_hbm, out_w, out_m,
    emb, cent, energy, ch, zb, xg, xb, ucol, racc, co, cs, vb, vcol, rr, uz, wacc, wr, cacc, cfs, cfr,
    e_sem, t_sem, c_send, c_recv, v_send, v_recv, r_send, r_recv,
    z_send, z_recv, x_send, x_recv, y_send, y_recv, k_send, k_recv,
    u_send, u_recv, w_send, w_recv,
):
    n_z = n_dp // 2
    rows, width = emb.shape
    cents = cent.shape[0]
    block = cents // NB
    quarter = rows // n_cent
    part_rows = quarter // PIECES
    scale = 1.0 / (TAU * width)
    ratio = total_rows / total_cents
    d = lax.axis_index("dp")
    c = lax.axis_index("cent")
    z, x = d // 2, lax.rem(d, 2)
    y, core = c // 2, lax.rem(c, 2)
    dp_peers = [lax.rem(d + k, n_dp) for k in range(1, n_dp)]
    c_peers = [lax.rem(c + k, n_cent) for k in range(1, n_cent)]
    c_y = (1 - y) * 2 + core
    c_core = y * 2 + (1 - core)
    d_x = z * 2 + (1 - x)
    z_pair = z + 1 - 2 * lax.rem(z, 2)
    d_z = z_pair * 2 + x

    def block_at(t):
        pair = t // 2
        at_z = jnp.where(
            pair == 0, z, jnp.where(pair == 1, lax.rem(z + 2, n_z), jnp.where(pair == 2, 3 - z, z_pair))
        )
        return at_z * 2 + lax.rem(x + t + t // 6, 2)

    def remote(src, dst, ssem, rsem, dp, cn):
        return pltpu.make_async_remote_copy(
            src_ref=src, dst_ref=dst, send_sem=ssem, recv_sem=rsem,
            device_id={"dp": dp, "cent": cn}, device_id_type=MESH,
        )

    def cent_copy(b):
        at = pl.multiple_of(b * block, block)
        return pltpu.make_async_copy(
            cent_hbm.at[pl.ds(at, block)], cent.at[pl.ds(at, block)], t_sem.at[b]
        )

    emb_copy = pltpu.make_async_copy(emb_hbm, emb, e_sem)
    emb_copy.start()

    @pl.loop(0, NB)
    def _(t):
        cent_copy(block_at(t)).start()

    barrier = pltpu.get_barrier_semaphore()
    for peer in dp_peers:
        pl.semaphore_signal(barrier, inc=1, device_id={"dp": peer, "cent": c}, device_id_type=MESH)
    for peer in c_peers:
        pl.semaphore_signal(barrier, inc=1, device_id={"dp": d, "cent": peer}, device_id_type=MESH)

    emb_copy.wait()
    mine = pl.multiple_of(c * quarter, quarter)
    zb[z] = rms_rows(emb[pl.ds(mine, quarter), :]).astype(jnp.float32)
    pl.semaphore_wait(barrier, n_dp - 1 + n_cent - 1)

    low = z // 2
    first = z + 1 - 2 * low
    other = 2 * z - first
    last = 3 - 3 * low
    order = [first, 6 - z - first - last, last]
    middle = (z == 1) | (z == 2)
    edge = jnp.logical_not(middle)
    n_items = 3 * PIECES

    def rows_of(p):
        return pl.ds(p * part_rows, part_rows)

    def z_copy(src, p, to, way, k):
        part = zb.at[src, rows_of(p)]
        return remote(part, part, z_send.at[way, k], z_recv.at[src, p], to * 2 + x, c)

    def z_arrival(i):
        j, p = divmod(i, PIECES)
        z_copy(order[j], p, first, 0, 0).wait_recv()

    def z_step(k):
        j, p = divmod(k, PIECES)
        if j == 0:
            z_copy(z, p, first, 0, k).start()

        @pl.when(middle)
        def _():
            if j == 0:
                z_copy(z, p, other, 1, k).start()
            if j == 1:
                z_copy(order[0], p, other, 1, k).start()
                z_arrival(k)
                z_copy(order[1], p, first, 0, k).start()
            if j == 2:
                z_arrival(k)
                z_copy(order[2], p, other, 1, k).start()

    def z_drain():
        for p in range(PIECES):
            z_copy(z, p, first, 0, p).wait_send()

        @pl.when(middle)
        def _():
            for p in range(PIECES):
                z_copy(z, p, other, 1, p).wait_send()
                z_copy(z, p, other, 1, p + PIECES).wait_send()
                z_copy(z, p, first, 0, p + PIECES).wait_send()
                z_copy(z, p, other, 1, p + 2 * PIECES).wait_send()

    def x_copy(i):
        j, p = divmod(i, PIECES)
        return remote(
            zb.at[order[j], rows_of(p)], xg.at[order[j], c, rows_of(p)],
            x_send.at[i], x_recv.at[i], d_x, c,
        )

    def own_part(i, crossed):
        j, p = divmod(i, PIECES)
        return xg.at[order[j], c, rows_of(p)] if crossed else zb.at[order[j], rows_of(p)]

    def y_copy(i, crossed, who):
        j, p = divmod(i, PIECES)
        return remote(
            own_part(i, crossed), xg.at[order[j], who, rows_of(p)],
            y_send.at[i], y_recv.at[i], d, c_y,
        )

    def k_copy(i, crossed, who):
        j, p = divmod(i, PIECES)
        return remote(
            own_part(i, crossed), xg.at[order[j], who, rows_of(p)],
            k_send.at[i, 0], k_recv.at[i, 0], d, c_core,
        )

    def k_copy_y(i, who):
        j, p = divmod(i, PIECES)
        part = xg.at[order[j], who, rows_of(p)]
        return remote(part, part, k_send.at[i, 1], k_recv.at[i, 1], d, c_core)

    def spread(i, crossed):
        y_copy(i, crossed, c).start()
        k_copy(i, crossed, c).start()

    def crossing(j):
        return (None, middle, edge)[j], (None, edge, middle)[j]

    def stage_x(i):
        j = i // PIECES
        crossed, straight = crossing(j)
        if j == 0:
            z_arrival(i)
            x_copy(i).start()
        else:

            @pl.when(edge)
            def _():
                z_arrival(i)

            @pl.when(crossed)
            def _():
                x_copy(i).start()

            @pl.when(straight)
            def _():
                spread(i, False)

    def stage_y(i):
        j = i // PIECES

        def act():
            x_copy(i).wait()
            spread(i, True)

        if j == 0:
            act()
        else:
            pl.when(crossing(j)[0])(act)

    def stage_core(i):
        y_copy(i, True, c_y).wait()
        k_copy_y(i, c_y).start()

    def stage_done(i):
        k_copy(i, True, c_core).wait()
        k_copy_y(i, c_core).wait()

    def step(k):
        if k < n_items:
            z_step(k)
        if 0 <= k - 1 < n_items:
            stage_x(k - 1)
        if 0 <= k - 2 < n_items:
            stage_y(k - 2)
        if 0 <= k - 3 < n_items:
            stage_core(k - 3)

    def steps(where):
        for k in PLAN.get(where, ()):
            step(k)

    def steps_at(where, t):
        for at, ks in PLAN.get(where, {}).items():

            @pl.when(t == at)
            def _():
                for k in ks:
                    step(k)

    def unpack(j):
        for p in range(PIECES):
            stage_done(j * PIECES + p)
        at = order[j] * rows
        for k in range(1, n_cent):
            who = lax.rem(c + k, n_cent)
            xb[pl.ds(pl.multiple_of(at + who * quarter, quarter), quarter), :] = xg[
                order[j], who
            ].astype(jnp.bfloat16)
        own = pl.ds(pl.multiple_of(at + c * quarter, quarter), quarter)
        if j == 0:
            xb[own, :] = xg[order[j], c].astype(jnp.bfloat16)
        else:
            crossed, straight = crossing(j)

            @pl.when(crossed)
            def _():
                xb[own, :] = xg[order[j], c].astype(jnp.bfloat16)

            @pl.when(straight)
            def _():
                xb[own, :] = zb[order[j]].astype(jnp.bfloat16)

    steps("start")
    base = pl.multiple_of(z * rows, rows)
    for i in range(n_cent):
        xb[pl.ds(base + i * quarter, quarter), :] = rms_rows(emb[i * quarter : (i + 1) * quarter, :])

    def c_copy(it, b, owner):
        return remote(co.at[it, b], cs.at[it, owner], c_send.at[it, b], c_recv.at[it, owner], b, c)

    def v_copy(it, owner, to):
        part = vb.at[it, owner]
        return remote(part, part, v_send.at[it, to], v_recv.at[it, owner], to, c)

    def r_copy(it, k, owner):
        part = rr.at[it, owner]
        return remote(part, part, r_send.at[it, k], r_recv.at[it, owner], d, c_peers[k])

    def column_part(it, t, b, col):
        row = jnp.sum(col, axis=0, keepdims=True)

        @pl.when(t == 0)
        def _():
            cs[it, d] = row

        @pl.when(t > 0)
        def _():
            co[it, b] = row
            c_copy(it, b, d).start()

    def exchange(it):
        rr[it, c] = to_row(racc[...])
        for k in range(n_cent - 1):
            r_copy(it, k, c).start()
        for peer in dp_peers:
            c_copy(it, peer, peer).wait_recv()
        col_sum = cs[it, 0]
        for k in range(1, n_dp):
            col_sum = col_sum + cs[it, k]
        v_old = vb[it - 1, d] if it else jnp.ones((1, block), jnp.float32)
        vb[it, d] = jnp.sqrt(v_old * ratio / col_sum)
        if it < ITERS - 1:

            @pl.loop(1, NB)
            def _(t):
                v_copy(it, d, block_at(t)).start()
        else:
            v_copy(it, d, d_x).start()
            v_copy(it, d, d_z).start()
        steps("exchange%d" % it)
        for k, peer in enumerate(c_peers):
            r_copy(it, k, peer).wait()
        row_sum = rr[it, 0]
        for k in range(1, n_cent):
            row_sum = row_sum + rr[it, k]
        u_old = uz[z] if it else jnp.ones((1, rows), jnp.float32)
        u_new = jnp.sqrt(u_old / row_sum)
        uz[z] = u_new
        if it < ITERS - 1:
            ucol[...] = to_column(u_new)

    racc[...] = jnp.zeros_like(racc)

    @pl.loop(0, NB)
    def _(t):
        steps_at("scores", t)
        b = block_at(t)
        at = pl.multiple_of(b * block, block)
        cent_copy(b).wait()
        ch_b = rms_rows(cent[pl.ds(at, block), :])
        ch[pl.ds(at, block), :] = ch_b
        col = jnp.zeros((8, block), jnp.float32)
        for i in range(n_cent):
            part = slice(i * quarter, (i + 1) * quarter)
            s = lax.dot_general(
                xb[pl.ds(base + i * quarter, quarter), :], ch_b, NT,
                preferred_element_type=jnp.float32,
            )
            e = jnp.exp(s * scale)
            energy[b, part, :] = e
            racc[part, :] += lane_tiles(e)
            col = col + jnp.sum(e.reshape(quarter // 8, 8, block), axis=0)
        column_part(0, t, b, col)

    exchange(0)

    group = 64
    for it in range(1, ITERS):
        racc[...] = jnp.zeros_like(racc)

        @pl.loop(0, NB)
        def _(t):
            steps_at("pass%d" % it, t)
            b = block_at(t)

            @pl.when(t > 0)
            def _():
                v_copy(it - 1, b, d_x).wait_recv()

            v_b = jnp.broadcast_to(vb[it - 1, b], (8, block))

            def rows_step(g, col):
                r0 = pl.multiple_of(g * group, group)
                for i in range(group // 8):
                    e = energy[b, pl.ds(r0 + i * 8, 8), :]
                    u8 = ucol[pl.ds(r0 + i * 8, 8), :]
                    col = col + e * jnp.concatenate([u8] * (block // 128), axis=1)
                    racc[pl.ds(r0 + i * 8, 8), :] += lane_tiles(e * v_b)
                return col

            col = lax.fori_loop(0, rows // group, rows_step, jnp.zeros((8, block), jnp.float32))
            column_part(it, t, b, col)

        exchange(it)

    def u_copy(k, owner):
        to = lax.rem(z + k, n_z)
        return remote(
            uz.at[owner], uz.at[owner], u_send.at[k - 1], u_recv.at[owner],
            to * 2 + lax.rem(x + k, 2), c,
        )

    for k in range(1, n_z):
        u_copy(k, z).start()
    final = ITERS - 1
    v_copy(final, d_x, d_x).wait_recv()
    v_copy(final, d_z, d_z).wait_recv()
    owners = (d_x, d_z, d, d)
    for q, owner in enumerate(owners):
        s = q % 2
        vcol[q] = to_column(vb[final, owner][:, s * CHUNK : (s + 1) * CHUNK])
    wacc[...] = jnp.zeros_like(wacc)
    cacc[...] = jnp.zeros_like(cacc)
    steps("u")
    unpack(0)
    for k in range(1, n_z):
        u_copy(k, lax.rem(z + k, n_z)).wait()

    def weigh(q, src):
        owner = jnp.where(q == 0, d_x, jnp.where(q == 1, d_z, d))
        at = pl.multiple_of(owner * block + lax.rem(q, 2) * CHUNK, CHUNK)
        cc = ch[pl.ds(at, CHUNK), :]
        v_tile = jnp.concatenate([vcol[q]] * (block // 128), axis=1)
        for h in range(rows // block):
            xr = xb[pl.ds(pl.multiple_of(src * rows + h * block, block), block), :]
            u = uz[src][:, h * block : (h + 1) * block]
            e = jnp.exp(lax.dot_general(cc, xr, NT, preferred_element_type=jnp.float32) * scale)
            cacc[q] += lane_tiles(e * u)
            w = ((total_cents * u) * e * v_tile).astype(jnp.bfloat16)
            wacc[q] += jnp.dot(w, xr, preferred_element_type=jnp.float32)

    n_q = len(owners)

    @pl.loop(0, n_q * (n_z - 1))
    def _(t):
        steps_at("weigh", t)

        @pl.when(t == 2 * n_q)
        def _():
            unpack(1)

        j = t // n_q
        src = jnp.where(j == 0, z, jnp.where(j == 1, order[0], order[1]))
        weigh(lax.rem(t, n_q), src)

    steps("end")
    unpack(2)

    def w_copy(s):
        return remote(wacc.at[s], wr.at[s], w_send.at[s], w_recv.at[s], owners[s], c)

    def f_copy(s):
        return remote(cfs.at[s], cfr.at[s], w_send.at[2 + s], w_recv.at[2 + s], owners[s], c)

    @pl.loop(0, n_q)
    def _(q):
        weigh(q, order[2])
        cfs[q] = to_row(cacc[q])
        for s in range(2):

            @pl.when(q == s)
            def _():
                w_copy(s).start()
                f_copy(s).start()

    z_drain()
    for it in range(ITERS):

        @pl.loop(1, NB)
        def _(t):
            b = block_at(t)
            c_copy(it, b, d).wait_send()
            if it < final:
                v_copy(it, d, b).wait_send()

    v_copy(final, d, d_x).wait_send()
    v_copy(final, d, d_z).wait_send()
    for s in range(2):
        f_copy(s).wait()
        w_copy(s).wait()
        w = wacc[2 + s] + wr[s]
        out_w[s] = w * lax.rsqrt(jnp.mean(w * w, axis=1, keepdims=True) + 1e-06)
        half = slice(s * CHUNK, (s + 1) * CHUNK)
        out_m[:, half] = (
            vb[final, d][:, half] * (cfs[2 + s] + cfr[s]) * (total_cents / total_rows)
        )


def fused(embeddings, centroids):
    n_dp, n_cent = lax.axis_size("dp"), lax.axis_size("cent")
    rows, width = embeddings.shape
    cents = centroids.shape[0]
    n_z = n_dp // 2
    block = cents // NB
    quarter = rows // n_cent
    n_s = block // CHUNK
    n_items = 3 * PIECES
    f32 = jnp.float32
    dma = pltpu.SemaphoreType.DMA
    w, m = pl.pallas_call(
        functools.partial(
            kernel, float(rows * n_dp), float(cents * n_cent), n_dp, n_cent
        ),
        out_shape=(
            jax.ShapeDtypeStruct((n_s, CHUNK, width), f32),
            jax.ShapeDtypeStruct((1, block), f32),
        ),
        in_specs=[pl.BlockSpec(memory_space=pl.ANY)] * 2,
        out_specs=(pl.BlockSpec(memory_space=pltpu.VMEM),) * 2,
        scratch_shapes=[
            pltpu.VMEM((rows, width), jnp.bfloat16),
            pltpu.VMEM((cents, width), jnp.bfloat16),
            pltpu.VMEM((NB, rows, block), f32),
            pltpu.VMEM((cents, width), jnp.bfloat16),
            pltpu.VMEM((n_z, quarter, width), f32),
            pltpu.VMEM((n_z, n_cent, quarter, width), f32),
            pltpu.VMEM((n_z * rows, width), jnp.bfloat16),
            pltpu.VMEM((rows, 128), f32),
            pltpu.VMEM((rows, 128), f32),
            pltpu.VMEM((ITERS, NB, 1, block), f32),
            pltpu.VMEM((ITERS, n_dp, 1, block), f32),
            pltpu.VMEM((ITERS, n_dp, 1, block), f32),
            pltpu.VMEM((2 * n_s, CHUNK, 128), f32),
            pltpu.VMEM((ITERS, n_cent, 1, rows), f32),
            pltpu.VMEM((n_z, 1, rows), f32),
            pltpu.VMEM((2 * n_s, CHUNK, width), f32),
            pltpu.VMEM((n_s, CHUNK, width), f32),
            pltpu.VMEM((2 * n_s, CHUNK, 128), f32),
            pltpu.VMEM((2 * n_s, 1, CHUNK), f32),
            pltpu.VMEM((n_s, 1, CHUNK), f32),
            dma,
            dma((NB,)),
            dma((ITERS, n_dp)),
            dma((ITERS, n_dp)),
            dma((ITERS, n_dp)),
            dma((ITERS, n_dp)),
            dma((ITERS, n_cent - 1)),
            dma((ITERS, n_cent)),
            dma((2, n_items)),
            dma((n_z, PIECES)),
            dma((n_items,)),
            dma((n_items,)),
            dma((n_items,)),
            dma((n_items,)),
            dma((n_items, 2)),
            dma((n_items, 2)),
            dma((n_z - 1,)),
            dma((n_z,)),
            dma((2 * n_s,)),
            dma((2 * n_s,)),
        ],
        compiler_params=pltpu.CompilerParams(
            collective_id=0, has_side_effects=True, vmem_limit_bytes=60 * 2**20
        ),
    )(embeddings, centroids)
    return w.reshape(block, width), m.reshape(block)


def column_total(weights, energy):
    return lax.psum(jnp.dot(weights, energy, precision=lax.Precision.HIGHEST), "dp")


def local(embeddings, centroids):
    n_data = lax.axis_size("dp")
    xh = rms_rows(embeddings)
    ch = rms_rows(centroids)
    local_rows, width = xh.shape
    local_cents = ch.shape[0]
    total_rows = float(local_rows * n_data)
    total_cents = float(local_cents * lax.axis_size("cent"))
    scores = lax.dot_general(xh, ch, NT, preferred_element_type=jnp.float32)
    energy = jnp.exp(scores * (1.0 / (TAU * width)))
    u = jnp.ones((local_rows,), jnp.float32)
    v = jnp.ones((local_cents,), jnp.float32)
    for step_index in range(ITERS):
        rows_sum = lax.psum(jnp.dot(energy, v, precision=lax.Precision.HIGHEST), "cent")
        cols = column_total(u, energy)
        u, v = (jnp.sqrt(u / rows_sum), jnp.sqrt(v * (total_rows / total_cents) / cols))
    cols = column_total(u, energy)
    plan = (total_cents * u[:, None] * energy * v[None, :]).astype(jnp.bfloat16)
    share = local_cents // n_data
    weighted = lax.dot_general(
        plan, xh, (((0,), (0,)), ((), ())), preferred_element_type=jnp.float32
    )
    mine = lax.psum_scatter(weighted, "dp", scatter_dimension=0, tiled=True)
    mass_all = v * cols * (total_cents / total_rows)
    column_mass = lax.dynamic_slice_in_dim(mass_all, lax.axis_index("dp") * share, share, 0)
    new_centroids = mine * lax.rsqrt(jnp.mean(mine * mine, axis=1, keepdims=True) + 1e-06)
    return (new_centroids, column_mass)


def solution(mesh):
    in_specs = (P("dp", None), P("cent", None))
    out_specs = (P(("cent", "dp"), None), P(("cent", "dp")))
    small = mesh.shape["dp"] == NB and mesh.shape["cent"] == 4
    body = fused if small else local
    return jax.shard_map(body, mesh=mesh, in_specs=in_specs, out_specs=out_specs, check_vma=False)
```

```python
import functools
import jax
import jax.numpy as jnp
from jax import lax
from jax.experimental import pallas as pl
from jax.experimental.pallas import tpu as pltpu
from jax.sharding import PartitionSpec as P

ITERS = 3
TAU = 0.02
MESH = pl.DeviceIdType.MESH
NT = (((1,), (1,)), ((), ()))
NB = 8
CHUNK = 256
PIECES = 8
LAG_Y, LAG_CORE = 3, 6
PLAN = {
    "start": ((0, 1, 2, 3, 4, 5), ()),
    "scores": {3: ((), (0,)), 4: ((), (1,)), 5: ((), (2,)), 6: ((6,), (3,))},
    "sums0": ((7,), (4,)),
    "shared0": ((8, 9), (5, 6)),
    "pass1": {0: ((10,), (7,)), 2: ((11,), (8,)), 4: ((12,), (9,)), 6: ((), (10,))},
    "sums1": ((13,), (11,)),
    "shared1": ((14, 15), (12,)),
    "pass2": {0: ((16,), (13,)), 2: ((17,), (14,)), 5: ((), (15,))},
    "sums2": ((18,), (16,)),
    "shared2": ((19, 20), (17, 18)),
    "u": ((21,), (19,)),
    "weigh": {
        0: ((22, 23), (20, 21)), 2: ((), (22,)), 4: ((), (23,)), 5: ((), (24,)), 6: ((), (25,)),
        7: ((), (26,)), 8: ((), (27,)), 9: ((), (28,)), 10: ((), (29,)),
    },
}


def rms_rows(values):
    wide = values.astype(jnp.float32)
    return (wide * lax.rsqrt(jnp.mean(wide * wide, axis=1, keepdims=True) + 1e-06)).astype(
        jnp.bfloat16
    )


def lane_tiles(values):
    total = values[:, :128]
    for t in range(1, values.shape[1] // 128):
        total = total + values[:, t * 128 : (t + 1) * 128]
    return total


def to_column(row):
    return jnp.broadcast_to(row, (128, row.shape[1])).T


def to_row(tile):
    return jnp.sum(tile.T, axis=0, keepdims=True)


def kernel(
    total_rows, total_cents, n_dp, n_cent,
    emb_hbm, cent_hbm, out_w, out_m,
    emb, cent, energy, ch, zb, xg, xb, ucol, racc, co, cs, vb, vcol, rr, uz, wacc, wr, cacc, cfs, cfr,
    e_sem, t_sem, c_send, c_recv, v_send, v_recv, r_send, r_recv,
    z_send, z_recv, x_send, x_recv, y_send, y_recv, k_send, k_recv,
    u_send, u_recv, w_send, w_recv,
):
    n_z = n_dp // 2
    rows, width = emb.shape
    cents = cent.shape[0]
    block = cents // NB
    quarter = rows // n_cent
    part_rows = quarter // PIECES
    scale = 1.0 / (TAU * width)
    ratio = total_rows / total_cents
    d = lax.axis_index("dp")
    c = lax.axis_index("cent")
    z, x = d // 2, lax.rem(d, 2)
    y, core = c // 2, lax.rem(c, 2)
    dp_peers = [lax.rem(d + k, n_dp) for k in range(1, n_dp)]
    c_peers = [lax.rem(c + k, n_cent) for k in range(1, n_cent)]
    c_y = (1 - y) * 2 + core
    c_core = y * 2 + (1 - core)
    d_x = z * 2 + (1 - x)
    z_pair = z + 1 - 2 * lax.rem(z, 2)
    d_z = z_pair * 2 + x

    def block_at(t):
        pair = t // 2
        at_z = jnp.where(
            pair == 0, z, jnp.where(pair == 1, lax.rem(z + 2, n_z), jnp.where(pair == 2, 3 - z, z_pair))
        )
        return at_z * 2 + lax.rem(x + t + t // 6, 2)

    def remote(src, dst, ssem, rsem, dp, cn):
        return pltpu.make_async_remote_copy(
            src_ref=src, dst_ref=dst, send_sem=ssem, recv_sem=rsem,
            device_id={"dp": dp, "cent": cn}, device_id_type=MESH,
        )

    def cent_copy(b):
        at = pl.multiple_of(b * block, block)
        return pltpu.make_async_copy(
            cent_hbm.at[pl.ds(at, block)], cent.at[pl.ds(at, block)], t_sem.at[b]
        )

    emb_copy = pltpu.make_async_copy(emb_hbm, emb, e_sem)
    emb_copy.start()

    @pl.loop(0, NB)
    def _(t):
        cent_copy(block_at(t)).start()

    barrier = pltpu.get_barrier_semaphore()
    for peer in dp_peers:
        pl.semaphore_signal(barrier, inc=1, device_id={"dp": peer, "cent": c}, device_id_type=MESH)
    for peer in c_peers:
        pl.semaphore_signal(barrier, inc=1, device_id={"dp": d, "cent": peer}, device_id_type=MESH)

    emb_copy.wait()
    mine = pl.multiple_of(c * quarter, quarter)
    zb[z] = rms_rows(emb[pl.ds(mine, quarter), :]).astype(jnp.float32)
    pl.semaphore_wait(barrier, n_dp - 1 + n_cent - 1)

    low = z // 2
    first = z + 1 - 2 * low
    other = 2 * z - first
    last = 3 - 3 * low
    order = [first, 6 - z - first - last, last]
    middle = (z == 1) | (z == 2)
    edge = jnp.logical_not(middle)
    n_items = 3 * PIECES

    def rows_of(p):
        return pl.ds(p * part_rows, part_rows)

    def z_copy(src, p, to, way, k):
        part = zb.at[src, rows_of(p)]
        return remote(part, part, z_send.at[way, k], z_recv.at[src, p], to * 2 + x, c)

    def z_arrival(i):
        j, p = divmod(i, PIECES)
        z_copy(order[j], p, first, 0, 0).wait_recv()

    def z_step(k):
        j, p = divmod(k, PIECES)
        if j == 0:
            z_copy(z, p, first, 0, k).start()

        @pl.when(middle)
        def _():
            if j == 0:
                z_copy(z, p, other, 1, k).start()
            if j == 1:
                z_copy(order[0], p, other, 1, k).start()
                z_arrival(k)
                z_copy(order[1], p, first, 0, k).start()
            if j == 2:
                z_arrival(k)
                z_copy(order[2], p, other, 1, k).start()

    def z_drain():
        for p in range(PIECES):
            z_copy(z, p, first, 0, p).wait_send()

        @pl.when(middle)
        def _():
            for p in range(PIECES):
                z_copy(z, p, other, 1, p).wait_send()
                z_copy(z, p, other, 1, p + PIECES).wait_send()
                z_copy(z, p, first, 0, p + PIECES).wait_send()
                z_copy(z, p, other, 1, p + 2 * PIECES).wait_send()

    def x_copy(i):
        j, p = divmod(i, PIECES)
        return remote(
            zb.at[order[j], rows_of(p)], xg.at[order[j], c, rows_of(p)],
            x_send.at[i], x_recv.at[i], d_x, c,
        )

    def own_part(i, crossed):
        j, p = divmod(i, PIECES)
        return xg.at[order[j], c, rows_of(p)] if crossed else zb.at[order[j], rows_of(p)]

    def y_copy(i, crossed, who):
        j, p = divmod(i, PIECES)
        return remote(
            own_part(i, crossed), xg.at[order[j], who, rows_of(p)],
            y_send.at[i], y_recv.at[i], d, c_y,
        )

    def k_copy(i, crossed, who):
        j, p = divmod(i, PIECES)
        return remote(
            own_part(i, crossed), xg.at[order[j], who, rows_of(p)],
            k_send.at[i, 0], k_recv.at[i, 0], d, c_core,
        )

    def k_copy_y(i, who):
        j, p = divmod(i, PIECES)
        part = xg.at[order[j], who, rows_of(p)]
        return remote(part, part, k_send.at[i, 1], k_recv.at[i, 1], d, c_core)

    def spread(i, crossed):
        y_copy(i, crossed, c).start()
        k_copy(i, crossed, c).start()

    def crossing(j):
        return (None, middle, edge)[j], (None, edge, middle)[j]

    def stage_x(i):
        j = i // PIECES
        if j == 0:
            z_arrival(i)
            x_copy(i).start()
        else:

            @pl.when(edge)
            def _():
                z_arrival(i)

            @pl.when(crossing(j)[0])
            def _():
                x_copy(i).start()

    def stage_y(i):
        j = i // PIECES

        def across():
            x_copy(i).wait()
            spread(i, True)

        if j == 0:
            across()
        else:
            crossed, straight = crossing(j)
            pl.when(crossed)(across)

            @pl.when(straight)
            def _():
                spread(i, False)

    def stage_core(i):
        y_copy(i, True, c_y).wait()
        k_copy_y(i, c_y).start()

    def stage_done(i):
        k_copy(i, True, c_core).wait()
        k_copy_y(i, c_core).wait()

    def step(plan):
        for k in plan[0]:
            z_step(k)
        for k in plan[1]:
            if 0 <= k < n_items:
                stage_x(k)
            if 0 <= k - LAG_Y < n_items:
                stage_y(k - LAG_Y)
            if 0 <= k - LAG_CORE < n_items:
                stage_core(k - LAG_CORE)

    def steps(where):
        step(PLAN[where])

    def steps_at(where, t):
        for at, plan in PLAN[where].items():

            @pl.when(t == at)
            def _():
                step(plan)

    def unpack(j):
        for p in range(PIECES):
            stage_done(j * PIECES + p)
        at = order[j] * rows
        for k in range(1, n_cent):
            who = lax.rem(c + k, n_cent)
            xb[pl.ds(pl.multiple_of(at + who * quarter, quarter), quarter), :] = xg[
                order[j], who
            ].astype(jnp.bfloat16)
        own = pl.ds(pl.multiple_of(at + c * quarter, quarter), quarter)
        if j == 0:
            xb[own, :] = xg[order[j], c].astype(jnp.bfloat16)
        else:
            crossed, straight = crossing(j)

            @pl.when(crossed)
            def _():
                xb[own, :] = xg[order[j], c].astype(jnp.bfloat16)

            @pl.when(straight)
            def _():
                xb[own, :] = zb[order[j]].astype(jnp.bfloat16)

    steps("start")
    base = pl.multiple_of(z * rows, rows)
    for i in range(n_cent):
        xb[pl.ds(base + i * quarter, quarter), :] = rms_rows(emb[i * quarter : (i + 1) * quarter, :])

    def c_copy(it, b, owner):
        return remote(co.at[it, b], cs.at[it, owner], c_send.at[it, b], c_recv.at[it, owner], b, c)

    def v_copy(it, owner, to):
        part = vb.at[it, owner]
        return remote(part, part, v_send.at[it, to], v_recv.at[it, owner], to, c)

    def r_copy(it, k, owner):
        part = rr.at[it, owner]
        return remote(part, part, r_send.at[it, k], r_recv.at[it, owner], d, c_peers[k])

    def column_part(it, t, b, col):
        row = jnp.sum(col, axis=0, keepdims=True)

        @pl.when(t == 0)
        def _():
            cs[it, d] = row

        @pl.when(t > 0)
        def _():
            co[it, b] = row
            c_copy(it, b, d).start()

    def exchange(it):
        rr[it, c] = to_row(racc[...])
        for k in range(n_cent - 1):
            r_copy(it, k, c).start()
        steps("sums%d" % it)
        for peer in dp_peers:
            c_copy(it, peer, peer).wait_recv()
        col_sum = cs[it, 0]
        for k in range(1, n_dp):
            col_sum = col_sum + cs[it, k]
        v_old = vb[it - 1, d] if it else jnp.ones((1, block), jnp.float32)
        vb[it, d] = jnp.sqrt(v_old * ratio / col_sum)
        if it < ITERS - 1:

            @pl.loop(1, NB)
            def _(t):
                v_copy(it, d, block_at(t)).start()
        else:
            v_copy(it, d, d_x).start()
            v_copy(it, d, d_z).start()
        steps("shared%d" % it)
        for k, peer in enumerate(c_peers):
            r_copy(it, k, peer).wait()
        row_sum = rr[it, 0]
        for k in range(1, n_cent):
            row_sum = row_sum + rr[it, k]
        u_old = uz[z] if it else jnp.ones((1, rows), jnp.float32)
        u_new = jnp.sqrt(u_old / row_sum)
        uz[z] = u_new
        if it < ITERS - 1:
            ucol[...] = to_column(u_new)

    racc[...] = jnp.zeros_like(racc)

    @pl.loop(0, NB)
    def _(t):
        steps_at("scores", t)
        b = block_at(t)
        at = pl.multiple_of(b * block, block)
        cent_copy(b).wait()
        ch_b = rms_rows(cent[pl.ds(at, block), :])
        ch[pl.ds(at, block), :] = ch_b
        col = jnp.zeros((8, block), jnp.float32)
        for i in range(n_cent):
            part = slice(i * quarter, (i + 1) * quarter)
            s = lax.dot_general(
                xb[pl.ds(base + i * quarter, quarter), :], ch_b, NT,
                preferred_element_type=jnp.float32,
            )
            e = jnp.exp(s * scale)
            energy[b, part, :] = e
            racc[part, :] += lane_tiles(e)
            col = col + jnp.sum(e.reshape(quarter // 8, 8, block), axis=0)
        column_part(0, t, b, col)

    exchange(0)

    group = 64
    for it in range(1, ITERS):
        racc[...] = jnp.zeros_like(racc)

        @pl.loop(0, NB)
        def _(t):
            steps_at("pass%d" % it, t)
            b = block_at(t)

            @pl.when(t > 0)
            def _():
                v_copy(it - 1, b, d_x).wait_recv()

            v_b = jnp.broadcast_to(vb[it - 1, b], (8, block))

            def rows_step(g, col):
                r0 = pl.multiple_of(g * group, group)
                for i in range(group // 8):
                    e = energy[b, pl.ds(r0 + i * 8, 8), :]
                    u8 = ucol[pl.ds(r0 + i * 8, 8), :]
                    col = col + e * jnp.concatenate([u8] * (block // 128), axis=1)
                    racc[pl.ds(r0 + i * 8, 8), :] += lane_tiles(e * v_b)
                return col

            col = lax.fori_loop(0, rows // group, rows_step, jnp.zeros((8, block), jnp.float32))
            column_part(it, t, b, col)

        exchange(it)

    def u_copy(k, owner):
        to = lax.rem(z + k, n_z)
        return remote(
            uz.at[owner], uz.at[owner], u_send.at[k - 1], u_recv.at[owner],
            to * 2 + lax.rem(x + k, 2), c,
        )

    for k in range(1, n_z):
        u_copy(k, z).start()
    final = ITERS - 1
    v_copy(final, d_x, d_x).wait_recv()
    v_copy(final, d_z, d_z).wait_recv()
    owners = (d_x, d_z, d, d)
    for q, owner in enumerate(owners):
        s = q % 2
        vcol[q] = to_column(vb[final, owner][:, s * CHUNK : (s + 1) * CHUNK])
    wacc[...] = jnp.zeros_like(wacc)
    cacc[...] = jnp.zeros_like(cacc)
    steps("u")
    for k in range(1, n_z):
        u_copy(k, lax.rem(z + k, n_z)).wait()

    def weigh(q, src):
        owner = jnp.where(q == 0, d_x, jnp.where(q == 1, d_z, d))
        at = pl.multiple_of(owner * block + lax.rem(q, 2) * CHUNK, CHUNK)
        cc = ch[pl.ds(at, CHUNK), :]
        v_tile = jnp.concatenate([vcol[q]] * (block // 128), axis=1)
        for h in range(rows // block):
            xr = xb[pl.ds(pl.multiple_of(src * rows + h * block, block), block), :]
            u = uz[src][:, h * block : (h + 1) * block]
            e = jnp.exp(lax.dot_general(cc, xr, NT, preferred_element_type=jnp.float32) * scale)
            cacc[q] += lane_tiles(e * u)
            w = ((total_cents * u) * e * v_tile).astype(jnp.bfloat16)
            wacc[q] += jnp.dot(w, xr, preferred_element_type=jnp.float32)

    n_q = len(owners)

    @pl.loop(0, n_q * (n_z - 1))
    def _(t):
        steps_at("weigh", t)

        @pl.when(t == n_q)
        def _():
            unpack(0)

        @pl.when(t == 2 * n_q)
        def _():
            unpack(1)

        j = t // n_q
        src = jnp.where(j == 0, z, jnp.where(j == 1, order[0], order[1]))
        weigh(lax.rem(t, n_q), src)

    unpack(2)

    def w_copy(s):
        return remote(wacc.at[s], wr.at[s], w_send.at[s], w_recv.at[s], owners[s], c)

    def f_copy(s):
        return remote(cfs.at[s], cfr.at[s], w_send.at[2 + s], w_recv.at[2 + s], owners[s], c)

    @pl.loop(0, n_q)
    def _(q):
        weigh(q, order[2])
        cfs[q] = to_row(cacc[q])
        for s in range(2):

            @pl.when(q == s)
            def _():
                w_copy(s).start()
                f_copy(s).start()

    z_drain()
    for it in range(ITERS):

        @pl.loop(1, NB)
        def _(t):
            b = block_at(t)
            c_copy(it, b, d).wait_send()
            if it < final:
                v_copy(it, d, b).wait_send()

    v_copy(final, d, d_x).wait_send()
    v_copy(final, d, d_z).wait_send()
    for s in range(2):
        f_copy(s).wait()
        w_copy(s).wait()
        w = wacc[2 + s] + wr[s]
        out_w[s] = w * lax.rsqrt(jnp.mean(w * w, axis=1, keepdims=True) + 1e-06)
        half = slice(s * CHUNK, (s + 1) * CHUNK)
        out_m[:, half] = (
            vb[final, d][:, half] * (cfs[2 + s] + cfr[s]) * (total_cents / total_rows)
        )


def fused(embeddings, centroids):
    n_dp, n_cent = lax.axis_size("dp"), lax.axis_size("cent")
    rows, width = embeddings.shape
    cents = centroids.shape[0]
    n_z = n_dp // 2
    block = cents // NB
    quarter = rows // n_cent
    n_s = block // CHUNK
    n_items = 3 * PIECES
    f32 = jnp.float32
    dma = pltpu.SemaphoreType.DMA
    w, m = pl.pallas_call(
        functools.partial(
            kernel, float(rows * n_dp), float(cents * n_cent), n_dp, n_cent
        ),
        out_shape=(
            jax.ShapeDtypeStruct((n_s, CHUNK, width), f32),
            jax.ShapeDtypeStruct((1, block), f32),
        ),
        in_specs=[pl.BlockSpec(memory_space=pl.ANY)] * 2,
        out_specs=(pl.BlockSpec(memory_space=pltpu.VMEM),) * 2,
        scratch_shapes=[
            pltpu.VMEM((rows, width), jnp.bfloat16),
            pltpu.VMEM((cents, width), jnp.bfloat16),
            pltpu.VMEM((NB, rows, block), f32),
            pltpu.VMEM((cents, width), jnp.bfloat16),
            pltpu.VMEM((n_z, quarter, width), f32),
            pltpu.VMEM((n_z, n_cent, quarter, width), f32),
            pltpu.VMEM((n_z * rows, width), jnp.bfloat16),
            pltpu.VMEM((rows, 128), f32),
            pltpu.VMEM((rows, 128), f32),
            pltpu.VMEM((ITERS, NB, 1, block), f32),
            pltpu.VMEM((ITERS, n_dp, 1, block), f32),
            pltpu.VMEM((ITERS, n_dp, 1, block), f32),
            pltpu.VMEM((2 * n_s, CHUNK, 128), f32),
            pltpu.VMEM((ITERS, n_cent, 1, rows), f32),
            pltpu.VMEM((n_z, 1, rows), f32),
            pltpu.VMEM((2 * n_s, CHUNK, width), f32),
            pltpu.VMEM((n_s, CHUNK, width), f32),
            pltpu.VMEM((2 * n_s, CHUNK, 128), f32),
            pltpu.VMEM((2 * n_s, 1, CHUNK), f32),
            pltpu.VMEM((n_s, 1, CHUNK), f32),
            dma,
            dma((NB,)),
            dma((ITERS, n_dp)),
            dma((ITERS, n_dp)),
            dma((ITERS, n_dp)),
            dma((ITERS, n_dp)),
            dma((ITERS, n_cent - 1)),
            dma((ITERS, n_cent)),
            dma((2, n_items)),
            dma((n_z, PIECES)),
            dma((n_items,)),
            dma((n_items,)),
            dma((n_items,)),
            dma((n_items,)),
            dma((n_items, 2)),
            dma((n_items, 2)),
            dma((n_z - 1,)),
            dma((n_z,)),
            dma((2 * n_s,)),
            dma((2 * n_s,)),
        ],
        compiler_params=pltpu.CompilerParams(
            collective_id=0, has_side_effects=True, vmem_limit_bytes=60 * 2**20
        ),
    )(embeddings, centroids)
    return w.reshape(block, width), m.reshape(block)


def column_total(weights, energy):
    return lax.psum(jnp.dot(weights, energy, precision=lax.Precision.HIGHEST), "dp")


def local(embeddings, centroids):
    n_data = lax.axis_size("dp")
    xh = rms_rows(embeddings)
    ch = rms_rows(centroids)
    local_rows, width = xh.shape
    local_cents = ch.shape[0]
    total_rows = float(local_rows * n_data)
    total_cents = float(local_cents * lax.axis_size("cent"))
    scores = lax.dot_general(xh, ch, NT, preferred_element_type=jnp.float32)
    energy = jnp.exp(scores * (1.0 / (TAU * width)))
    u = jnp.ones((local_rows,), jnp.float32)
    v = jnp.ones((local_cents,), jnp.float32)
    for step_index in range(ITERS):
        rows_sum = lax.psum(jnp.dot(energy, v, precision=lax.Precision.HIGHEST), "cent")
        cols = column_total(u, energy)
        u, v = (jnp.sqrt(u / rows_sum), jnp.sqrt(v * (total_rows / total_cents) / cols))
    cols = column_total(u, energy)
    plan = (total_cents * u[:, None] * energy * v[None, :]).astype(jnp.bfloat16)
    share = local_cents // n_data
    weighted = lax.dot_general(
        plan, xh, (((0,), (0,)), ((), ())), preferred_element_type=jnp.float32
    )
    mine = lax.psum_scatter(weighted, "dp", scatter_dimension=0, tiled=True)
    mass_all = v * cols * (total_cents / total_rows)
    column_mass = lax.dynamic_slice_in_dim(mass_all, lax.axis_index("dp") * share, share, 0)
    new_centroids = mine * lax.rsqrt(jnp.mean(mine * mine, axis=1, keepdims=True) + 1e-06)
    return (new_centroids, column_mass)


def solution(mesh):
    in_specs = (P("dp", None), P("cent", None))
    out_specs = (P(("cent", "dp"), None), P(("cent", "dp")))
    small = mesh.shape["dp"] == NB and mesh.shape["cent"] == 4
    body = fused if small else local
    return jax.shard_map(body, mesh=mesh, in_specs=in_specs, out_specs=out_specs, check_vma=False)
```

```python
import functools
import jax
import jax.numpy as jnp
from jax import lax
from jax.experimental import pallas as pl
from jax.experimental.pallas import tpu as pltpu
from jax.sharding import PartitionSpec as P

ITERS = 3
TAU = 0.02
MESH = pl.DeviceIdType.MESH
NT = (((1,), (1,)), ((), ()))
NB = 8
CHUNK = 256
PIECES = 8
LAG_Y, LAG_CORE = 3, 6
AHEAD = 0
PLAN = {
    "start": ((0, 1, 2, 3, 4, 5), ()),
    "scores": {3: ((), (0,)), 4: ((), (1,)), 5: ((), (2,)), 6: ((6,), (3,))},
    "sums0": ((7,), (4,)),
    "shared0": ((8, 9), (5, 6)),
    "pass1": {0: ((10,), (7,)), 2: ((11,), (8,)), 4: ((12,), (9,)), 6: ((), (10,))},
    "sums1": ((13,), (11,)),
    "shared1": ((14, 15), (12,)),
    "pass2": {0: ((16,), (13,)), 2: ((17,), (14,)), 5: ((), (15,))},
    "sums2": ((18,), (16,)),
    "shared2": ((19, 20), (17, 18)),
    "u": ((21,), (19,)),
    "weigh": {0: ((22, 23), (20, 21)), 1: ((), (22, 23)), 2: ((), (24,)), 3: ((), (25,)), 4: ((), (26, 27)), 5: ((), (28, 29))},
}


def rms_rows(values):
    wide = values.astype(jnp.float32)
    return (wide * lax.rsqrt(jnp.mean(wide * wide, axis=1, keepdims=True) + 1e-06)).astype(
        jnp.bfloat16
    )


def lane_tiles(values):
    total = values[:, :128]
    for t in range(1, values.shape[1] // 128):
        total = total + values[:, t * 128 : (t + 1) * 128]
    return total


def to_column(row):
    return jnp.broadcast_to(row, (128, row.shape[1])).T


def to_row(tile):
    return jnp.sum(tile.T, axis=0, keepdims=True)


def kernel(
    total_rows, total_cents, n_dp, n_cent,
    emb_hbm, cent_hbm, out_w, out_m,
    emb, cent, energy, ch, zb, xg, xb, ucol, racc, co, cs, vb, vcol, rr, uz, wacc, wr, cacc, cfs, cfr,
    e_sem, t_sem, c_send, c_recv, v_send, v_recv, r_send, r_recv,
    z_send, z_recv, x_send, x_recv, y_send, y_recv, k_send, k_recv,
    u_send, u_recv, w_send, w_recv,
):
    n_z = n_dp // 2
    rows, width = emb.shape
    cents = cent.shape[0]
    block = cents // NB
    quarter = rows // n_cent
    part_rows = quarter // PIECES
    scale = 1.0 / (TAU * width)
    ratio = total_rows / total_cents
    d = lax.axis_index("dp")
    c = lax.axis_index("cent")
    z, x = d // 2, lax.rem(d, 2)
    y, core = c // 2, lax.rem(c, 2)
    dp_peers = [lax.rem(d + k, n_dp) for k in range(1, n_dp)]
    c_peers = [lax.rem(c + k, n_cent) for k in range(1, n_cent)]
    c_y = (1 - y) * 2 + core
    c_core = y * 2 + (1 - core)
    d_x = z * 2 + (1 - x)
    z_pair = z + 1 - 2 * lax.rem(z, 2)
    d_z = z_pair * 2 + x

    def block_at(t):
        pair = t // 2
        at_z = jnp.where(
            pair == 0, z, jnp.where(pair == 1, lax.rem(z + 2, n_z), jnp.where(pair == 2, 3 - z, z_pair))
        )
        return at_z * 2 + lax.rem(x + t + t // 6, 2)

    def remote(src, dst, ssem, rsem, dp, cn):
        return pltpu.make_async_remote_copy(
            src_ref=src, dst_ref=dst, send_sem=ssem, recv_sem=rsem,
            device_id={"dp": dp, "cent": cn}, device_id_type=MESH,
        )

    def cent_copy(b):
        at = pl.multiple_of(b * block, block)
        return pltpu.make_async_copy(
            cent_hbm.at[pl.ds(at, block)], cent.at[pl.ds(at, block)], t_sem.at[b]
        )

    emb_copy = pltpu.make_async_copy(emb_hbm, emb, e_sem)
    emb_copy.start()

    @pl.loop(0, NB)
    def _(t):
        cent_copy(block_at(t)).start()

    barrier = pltpu.get_barrier_semaphore()
    for peer in dp_peers:
        pl.semaphore_signal(barrier, inc=1, device_id={"dp": peer, "cent": c}, device_id_type=MESH)
    for peer in c_peers:
        pl.semaphore_signal(barrier, inc=1, device_id={"dp": d, "cent": peer}, device_id_type=MESH)

    emb_copy.wait()
    mine = pl.multiple_of(c * quarter, quarter)
    zb[z] = rms_rows(emb[pl.ds(mine, quarter), :]).astype(jnp.float32)
    pl.semaphore_wait(barrier, n_dp - 1 + n_cent - 1)

    low = z // 2
    first = z + 1 - 2 * low
    other = 2 * z - first
    last = 3 - 3 * low
    order = [first, 6 - z - first - last, last]
    middle = (z == 1) | (z == 2)
    edge = jnp.logical_not(middle)
    n_items = 3 * PIECES

    def rows_of(p):
        return pl.ds(p * part_rows, part_rows)

    def z_copy(src, p, to, way, k):
        part = zb.at[src, rows_of(p)]
        return remote(part, part, z_send.at[way, k], z_recv.at[src, p], to * 2 + x, c)

    def z_arrival(i):
        j, p = divmod(i, PIECES)
        z_copy(order[j], p, first, 0, 0).wait_recv()

    def z_step(k):
        j, p = divmod(k, PIECES)
        if j == 0:
            z_copy(z, p, first, 0, k).start()

        @pl.when(middle)
        def _():
            if j == 0:
                z_copy(z, p, other, 1, k).start()
            if j == 1:
                z_copy(order[0], p, other, 1, k).start()
                z_arrival(k)
                z_copy(order[1], p, first, 0, k).start()
            if j == 2:
                z_arrival(k)
                z_copy(order[2], p, other, 1, k).start()

    def z_drain():
        for p in range(PIECES):
            z_copy(z, p, first, 0, p).wait_send()

        @pl.when(middle)
        def _():
            for p in range(PIECES):
                z_copy(z, p, other, 1, p).wait_send()
                z_copy(z, p, other, 1, p + PIECES).wait_send()
                z_copy(z, p, first, 0, p + PIECES).wait_send()
                z_copy(z, p, other, 1, p + 2 * PIECES).wait_send()

    def x_copy(i):
        j, p = divmod(i, PIECES)
        return remote(
            zb.at[order[j], rows_of(p)], xg.at[order[j], c, rows_of(p)],
            x_send.at[i], x_recv.at[i], d_x, c,
        )

    def own_part(i, crossed):
        j, p = divmod(i, PIECES)
        return xg.at[order[j], c, rows_of(p)] if crossed else zb.at[order[j], rows_of(p)]

    def y_copy(i, crossed, who):
        j, p = divmod(i, PIECES)
        return remote(
            own_part(i, crossed), xg.at[order[j], who, rows_of(p)],
            y_send.at[i], y_recv.at[i], d, c_y,
        )

    def k_copy(i, crossed, who):
        j, p = divmod(i, PIECES)
        return remote(
            own_part(i, crossed), xg.at[order[j], who, rows_of(p)],
            k_send.at[i, 0], k_recv.at[i, 0], d, c_core,
        )

    def k_copy_y(i, who):
        j, p = divmod(i, PIECES)
        part = xg.at[order[j], who, rows_of(p)]
        return remote(part, part, k_send.at[i, 1], k_recv.at[i, 1], d, c_core)

    def spread(i, crossed):
        y_copy(i, crossed, c).start()
        k_copy(i, crossed, c).start()

    def crossing(j):
        return (None, middle, edge)[j], (None, edge, middle)[j]

    def stage_x(i):
        j = i // PIECES
        if j == 0:
            z_arrival(i)
            x_copy(i).start()
        else:

            @pl.when(edge)
            def _():
                z_arrival(i)

            @pl.when(crossing(j)[0])
            def _():
                x_copy(i).start()

    def stage_y(i):
        j = i // PIECES

        def across():
            x_copy(i).wait()
            spread(i, True)

        if j == 0:
            across()
        else:
            crossed, straight = crossing(j)
            pl.when(crossed)(across)

            @pl.when(straight)
            def _():
                spread(i, False)

    def stage_core(i):
        y_copy(i, True, c_y).wait()
        k_copy_y(i, c_y).start()

    def stage_done(i):
        k_copy(i, True, c_core).wait()
        k_copy_y(i, c_core).wait()

    def step(plan):
        for k in plan[0]:
            z_step(k)
        for k in plan[1]:
            if 0 <= k < n_items:
                stage_x(k)
            if 0 <= k - LAG_Y < n_items:
                stage_y(k - LAG_Y)
            if 0 <= k - LAG_CORE < n_items:
                stage_core(k - LAG_CORE)

    def steps(where):
        step(PLAN[where])

    def steps_at(where, t):
        for at, plan in PLAN[where].items():

            @pl.when(t == at)
            def _():
                step(plan)

    def unpack(j):
        for p in range(PIECES):
            stage_done(j * PIECES + p)
        at = order[j] * rows
        for k in range(1, n_cent):
            who = lax.rem(c + k, n_cent)
            xb[pl.ds(pl.multiple_of(at + who * quarter, quarter), quarter), :] = xg[
                order[j], who
            ].astype(jnp.bfloat16)
        own = pl.ds(pl.multiple_of(at + c * quarter, quarter), quarter)
        if j == 0:
            xb[own, :] = xg[order[j], c].astype(jnp.bfloat16)
        else:
            crossed, straight = crossing(j)

            @pl.when(crossed)
            def _():
                xb[own, :] = xg[order[j], c].astype(jnp.bfloat16)

            @pl.when(straight)
            def _():
                xb[own, :] = zb[order[j]].astype(jnp.bfloat16)

    steps("start")
    base = pl.multiple_of(z * rows, rows)
    for i in range(n_cent):
        xb[pl.ds(base + i * quarter, quarter), :] = rms_rows(emb[i * quarter : (i + 1) * quarter, :])

    def c_copy(it, b, owner):
        return remote(co.at[it, b], cs.at[it, owner], c_send.at[it, b], c_recv.at[it, owner], b, c)

    def v_copy(it, owner, to):
        part = vb.at[it, owner]
        return remote(part, part, v_send.at[it, to], v_recv.at[it, owner], to, c)

    def r_copy(it, k, owner):
        part = rr.at[it, owner]
        return remote(part, part, r_send.at[it, k], r_recv.at[it, owner], d, c_peers[k])

    def column_part(it, t, b, col):
        row = jnp.sum(col, axis=0, keepdims=True)

        @pl.when(t == 0)
        def _():
            cs[it, d] = row

        @pl.when(t > 0)
        def _():
            co[it, b] = row
            c_copy(it, b, d).start()

    def exchange(it):
        rr[it, c] = to_row(racc[...])
        for k in range(n_cent - 1):
            r_copy(it, k, c).start()
        steps("sums%d" % it)
        for peer in dp_peers:
            c_copy(it, peer, peer).wait_recv()
        col_sum = cs[it, 0]
        for k in range(1, n_dp):
            col_sum = col_sum + cs[it, k]
        v_old = vb[it - 1, d] if it else jnp.ones((1, block), jnp.float32)
        vb[it, d] = jnp.sqrt(v_old * ratio / col_sum)
        if it < ITERS - 1:

            @pl.loop(1, NB)
            def _(t):
                v_copy(it, d, block_at(t)).start()
        else:
            v_copy(it, d, d_x).start()
            v_copy(it, d, d_z).start()
        steps("shared%d" % it)
        for k, peer in enumerate(c_peers):
            r_copy(it, k, peer).wait()
        row_sum = rr[it, 0]
        for k in range(1, n_cent):
            row_sum = row_sum + rr[it, k]
        u_old = uz[z] if it else jnp.ones((1, rows), jnp.float32)
        u_new = jnp.sqrt(u_old / row_sum)
        uz[z] = u_new
        if it < ITERS - 1:
            ucol[...] = to_column(u_new)

    racc[...] = jnp.zeros_like(racc)

    @pl.loop(0, NB)
    def _(t):
        steps_at("scores", t)
        b = block_at(t)
        at = pl.multiple_of(b * block, block)
        cent_copy(b).wait()
        ch_b = rms_rows(cent[pl.ds(at, block), :])
        ch[pl.ds(at, block), :] = ch_b
        col = jnp.zeros((8, block), jnp.float32)
        for i in range(n_cent):
            part = slice(i * quarter, (i + 1) * quarter)
            s = lax.dot_general(
                xb[pl.ds(base + i * quarter, quarter), :], ch_b, NT,
                preferred_element_type=jnp.float32,
            )
            e = jnp.exp(s * scale)
            energy[b, part, :] = e
            racc[part, :] += lane_tiles(e)
            col = col + jnp.sum(e.reshape(quarter // 8, 8, block), axis=0)
        column_part(0, t, b, col)

    exchange(0)

    group = 64
    for it in range(1, ITERS):
        racc[...] = jnp.zeros_like(racc)

        @pl.loop(0, NB)
        def _(t):
            steps_at("pass%d" % it, t)
            b = block_at(t)

            @pl.when(t > 0)
            def _():
                v_copy(it - 1, b, d_x).wait_recv()

            v_b = jnp.broadcast_to(vb[it - 1, b], (8, block))

            def rows_step(g, col):
                r0 = pl.multiple_of(g * group, group)
                for i in range(group // 8):
                    e = energy[b, pl.ds(r0 + i * 8, 8), :]
                    u8 = ucol[pl.ds(r0 + i * 8, 8), :]
                    col = col + e * jnp.concatenate([u8] * (block // 128), axis=1)
                    racc[pl.ds(r0 + i * 8, 8), :] += lane_tiles(e * v_b)
                return col

            col = lax.fori_loop(0, rows // group, rows_step, jnp.zeros((8, block), jnp.float32))
            column_part(it, t, b, col)

        exchange(it)

    def u_copy(k, owner):
        to = lax.rem(z + k, n_z)
        return remote(
            uz.at[owner], uz.at[owner], u_send.at[k - 1], u_recv.at[owner],
            to * 2 + lax.rem(x + k, 2), c,
        )

    for k in range(1, n_z):
        u_copy(k, z).start()
    final = ITERS - 1
    owners = (d_x, d_z, d, d)

    def column_scales(qs):
        for q in qs:
            s = q % 2
            vcol[q] = to_column(vb[final, owners[q]][:, s * CHUNK : (s + 1) * CHUNK])

    column_scales((2, 3))
    wacc[...] = jnp.zeros_like(wacc)
    cacc[...] = jnp.zeros_like(cacc)
    steps("u")

    def weigh(q, blocks):
        owner = jnp.where(q == 0, d_x, jnp.where(q == 1, d_z, d))
        at = pl.multiple_of(owner * block + lax.rem(q, 2) * CHUNK, CHUNK)
        cc = ch[pl.ds(at, CHUNK), :]
        v_tile = jnp.concatenate([vcol[q]] * (block // 128), axis=1)
        for first_row, u in blocks:
            xr = xb[pl.ds(pl.multiple_of(first_row, block), block), :]
            e = jnp.exp(lax.dot_general(cc, xr, NT, preferred_element_type=jnp.float32) * scale)
            cacc[q] += lane_tiles(e * u)
            w = ((total_cents * u) * e * v_tile).astype(jnp.bfloat16)
            wacc[q] += jnp.dot(w, xr, preferred_element_type=jnp.float32)

    def whole(src):
        return [
            (src * rows + h * block, uz[src][:, h * block : (h + 1) * block])
            for h in range(rows // block)
        ]

    n_out = 2 * (n_z - 1)

    def unit(t):
        late = jnp.maximum(t - n_out, 0)
        j = jnp.where(t < n_out, t, late) // 2
        src = jnp.where(j == 0, z, jnp.where(j == 1, order[0], jnp.where(j == 2, order[1], order[2])))
        weigh(lax.rem(t, 2) + jnp.where(t < n_out, 0, 2), whole(src))

    @pl.loop(0, n_out + AHEAD)
    def _(t):
        steps_at("weigh", t)

        @pl.when(t == 0)
        def _():
            v_copy(final, d_x, d_x).wait_recv()
            v_copy(final, d_z, d_z).wait_recv()
            column_scales((0, 1))

        @pl.when(t == 2)
        def _():
            unpack(0)
            for k in range(1, n_z):
                u_copy(k, lax.rem(z + k, n_z)).wait()

        @pl.when(t == 4)
        def _():
            unpack(1)

        unit(t)

    unpack(2)

    def w_copy(s):
        return remote(wacc.at[s], wr.at[s], w_send.at[s], w_recv.at[s], owners[s], c)

    def f_copy(s):
        return remote(cfs.at[s], cfr.at[s], w_send.at[2 + s], w_recv.at[2 + s], owners[s], c)

    @pl.loop(0, 2)
    def _(q):
        weigh(q, whole(order[2]))
        cfs[q] = to_row(cacc[q])
        for s in range(2):

            @pl.when(q == s)
            def _():
                w_copy(s).start()
                f_copy(s).start()

    @pl.loop(n_out + AHEAD, n_out + 2 * n_z)
    def _(t):
        unit(t)

    for q in (2, 3):
        cfs[q] = to_row(cacc[q])
    z_drain()
    for it in range(ITERS):

        @pl.loop(1, NB)
        def _(t):
            b = block_at(t)
            c_copy(it, b, d).wait_send()
            if it < final:
                v_copy(it, d, b).wait_send()

    v_copy(final, d, d_x).wait_send()
    v_copy(final, d, d_z).wait_send()
    for s in range(2):
        f_copy(s).wait()
        w_copy(s).wait()
        w = wacc[2 + s] + wr[s]
        out_w[s] = w * lax.rsqrt(jnp.mean(w * w, axis=1, keepdims=True) + 1e-06)
        half = slice(s * CHUNK, (s + 1) * CHUNK)
        out_m[:, half] = (
            vb[final, d][:, half] * (cfs[2 + s] + cfr[s]) * (total_cents / total_rows)
        )


def fused(embeddings, centroids):
    n_dp, n_cent = lax.axis_size("dp"), lax.axis_size("cent")
    rows, width = embeddings.shape
    cents = centroids.shape[0]
    n_z = n_dp // 2
    block = cents // NB
    quarter = rows // n_cent
    n_s = block // CHUNK
    n_items = 3 * PIECES
    f32 = jnp.float32
    dma = pltpu.SemaphoreType.DMA
    w, m = pl.pallas_call(
        functools.partial(
            kernel, float(rows * n_dp), float(cents * n_cent), n_dp, n_cent
        ),
        out_shape=(
            pltpu.VMEM((n_s, CHUNK, width), f32),
            pltpu.VMEM((1, block), f32),
        ),
        in_specs=[pl.BlockSpec(memory_space=pl.ANY)] * 2,
        out_specs=(pl.BlockSpec(memory_space=pltpu.VMEM),) * 2,
        scratch_shapes=[
            pltpu.VMEM((rows, width), jnp.bfloat16),
            pltpu.VMEM((cents, width), jnp.bfloat16),
            pltpu.VMEM((NB, rows, block), f32),
            pltpu.VMEM((cents, width), jnp.bfloat16),
            pltpu.VMEM((n_z, quarter, width), f32),
            pltpu.VMEM((n_z, n_cent, quarter, width), f32),
            pltpu.VMEM((n_z * rows, width), jnp.bfloat16),
            pltpu.VMEM((rows, 128), f32),
            pltpu.VMEM((rows, 128), f32),
            pltpu.VMEM((ITERS, NB, 1, block), f32),
            pltpu.VMEM((ITERS, n_dp, 1, block), f32),
            pltpu.VMEM((ITERS, n_dp, 1, block), f32),
            pltpu.VMEM((2 * n_s, CHUNK, 128), f32),
            pltpu.VMEM((ITERS, n_cent, 1, rows), f32),
            pltpu.VMEM((n_z, 1, rows), f32),
            pltpu.VMEM((2 * n_s, CHUNK, width), f32),
            pltpu.VMEM((n_s, CHUNK, width), f32),
            pltpu.VMEM((2 * n_s, CHUNK, 128), f32),
            pltpu.VMEM((2 * n_s, 1, CHUNK), f32),
            pltpu.VMEM((n_s, 1, CHUNK), f32),
            dma,
            dma((NB,)),
            dma((ITERS, n_dp)),
            dma((ITERS, n_dp)),
            dma((ITERS, n_dp)),
            dma((ITERS, n_dp)),
            dma((ITERS, n_cent - 1)),
            dma((ITERS, n_cent)),
            dma((2, n_items)),
            dma((n_z, PIECES)),
            dma((n_items,)),
            dma((n_items,)),
            dma((n_items,)),
            dma((n_items,)),
            dma((n_items, 2)),
            dma((n_items, 2)),
            dma((n_z - 1,)),
            dma((n_z,)),
            dma((2 * n_s,)),
            dma((2 * n_s,)),
        ],
        compiler_params=pltpu.CompilerParams(
            collective_id=0, has_side_effects=True, vmem_limit_bytes=60 * 2**20
        ),
    )(embeddings, centroids)
    return w.reshape(block, width), m.reshape(block)


def column_total(weights, energy):
    return lax.psum(jnp.dot(weights, energy, precision=lax.Precision.HIGHEST), "dp")


def local(embeddings, centroids):
    n_data = lax.axis_size("dp")
    xh = rms_rows(embeddings)
    ch = rms_rows(centroids)
    local_rows, width = xh.shape
    local_cents = ch.shape[0]
    total_rows = float(local_rows * n_data)
    total_cents = float(local_cents * lax.axis_size("cent"))
    scores = lax.dot_general(xh, ch, NT, preferred_element_type=jnp.float32)
    energy = jnp.exp(scores * (1.0 / (TAU * width)))
    u = jnp.ones((local_rows,), jnp.float32)
    v = jnp.ones((local_cents,), jnp.float32)
    for step_index in range(ITERS):
        rows_sum = lax.psum(jnp.dot(energy, v, precision=lax.Precision.HIGHEST), "cent")
        cols = column_total(u, energy)
        u, v = (jnp.sqrt(u / rows_sum), jnp.sqrt(v * (total_rows / total_cents) / cols))
    cols = column_total(u, energy)
    plan = (total_cents * u[:, None] * energy * v[None, :]).astype(jnp.bfloat16)
    share = local_cents // n_data
    weighted = lax.dot_general(
        plan, xh, (((0,), (0,)), ((), ())), preferred_element_type=jnp.float32
    )
    mine = lax.psum_scatter(weighted, "dp", scatter_dimension=0, tiled=True)
    mass_all = v * cols * (total_cents / total_rows)
    column_mass = lax.dynamic_slice_in_dim(mass_all, lax.axis_index("dp") * share, share, 0)
    new_centroids = mine * lax.rsqrt(jnp.mean(mine * mine, axis=1, keepdims=True) + 1e-06)
    return (new_centroids, column_mass)


def solution(mesh):
    in_specs = (P("dp", None), P("cent", None))
    out_specs = (P(("cent", "dp"), None), P(("cent", "dp")))
    small = mesh.shape["dp"] == NB and mesh.shape["cent"] == 4
    body = fused if small else local
    return jax.shard_map(body, mesh=mesh, in_specs=in_specs, out_specs=out_specs, check_vma=False)
```

```python
import functools
import jax
import jax.numpy as jnp
from jax import lax
from jax.experimental import pallas as pl
from jax.experimental.pallas import tpu as pltpu
from jax.sharding import PartitionSpec as P

ITERS = 3
TAU = 0.02
MESH = pl.DeviceIdType.MESH
NT = (((1,), (1,)), ((), ()))
NB = 8
CHUNK = 256
PIECES = 8
LAG_Y, LAG_CORE = 3, 6
AHEAD = 0
PLAN = {
    "start": ((0, 1, 2, 3, 4, 5), ()),
    "scores": {3: ((), (0,)), 4: ((), (1,)), 5: ((6,), (2,)), 6: ((), (3,)), 7: ((7,), (4,))},
    "sums0": ((8,), (5,)),
    "shared0": ((9, 10), (6, 7)),
    "pass1": {0: ((11,), (8,)), 2: ((12,), (9,)), 3: ((), (10,)), 5: ((13,), (11,))},
    "sums1": ((14,), (12,)),
    "shared1": ((15, 16), (13, 14)),
    "pass2": {0: ((17,), (15,)), 2: ((18,), (16,)), 4: ((19,), (17,))},
    "sums2": ((20,), (18,)),
    "shared2": ((21, 22), (19, 20)),
    "u": ((23,), (21,)),
    "weigh": {0: ((), (22, 23)), 1: ((), (24,)), 2: ((), (25,)), 3: ((), (26,))},
}


def rms_rows(values):
    wide = values.astype(jnp.float32)
    return (wide * lax.rsqrt(jnp.mean(wide * wide, axis=1, keepdims=True) + 1e-06)).astype(
        jnp.bfloat16
    )


def lane_tiles(values):
    total = values[:, :128]
    for t in range(1, values.shape[1] // 128):
        total = total + values[:, t * 128 : (t + 1) * 128]
    return total


def to_column(row):
    return jnp.broadcast_to(row, (128, row.shape[1])).T


def to_row(tile):
    return jnp.sum(tile.T, axis=0, keepdims=True)


def kernel(
    total_rows, total_cents, n_dp, n_cent,
    emb_hbm, cent_hbm, out_w, out_m,
    emb, cent, energy, ch, zb, xg, xb, ucol, racc, co, cs, vb, vcol, rr, uz, wacc, wr, cacc, cfs, cfr,
    e_sem, t_sem, c_send, c_recv, v_send, v_recv, r_send, r_recv,
    z_send, z_recv, x_send, x_recv, y_send, y_recv, k_send, k_recv,
    u_send, u_recv, w_send, w_recv,
):
    n_z = n_dp // 2
    rows, width = emb.shape
    cents = cent.shape[0]
    block = cents // NB
    quarter = rows // n_cent
    part_rows = quarter // PIECES
    scale = 1.0 / (TAU * width)
    ratio = total_rows / total_cents
    d = lax.axis_index("dp")
    c = lax.axis_index("cent")
    z, x = d // 2, lax.rem(d, 2)
    y, core = c // 2, lax.rem(c, 2)
    dp_peers = [lax.rem(d + k, n_dp) for k in range(1, n_dp)]
    c_peers = [lax.rem(c + k, n_cent) for k in range(1, n_cent)]
    c_y = (1 - y) * 2 + core
    c_core = y * 2 + (1 - core)
    d_x = z * 2 + (1 - x)
    z_pair = z + 1 - 2 * lax.rem(z, 2)
    d_z = z_pair * 2 + x

    def block_at(t):
        pair = t // 2
        at_z = jnp.where(
            pair == 0, z, jnp.where(pair == 1, lax.rem(z + 2, n_z), jnp.where(pair == 2, 3 - z, z_pair))
        )
        return at_z * 2 + lax.rem(x + t + t // 6, 2)

    def remote(src, dst, ssem, rsem, dp, cn):
        return pltpu.make_async_remote_copy(
            src_ref=src, dst_ref=dst, send_sem=ssem, recv_sem=rsem,
            device_id={"dp": dp, "cent": cn}, device_id_type=MESH,
        )

    def cent_copy(b):
        at = pl.multiple_of(b * block, block)
        return pltpu.make_async_copy(
            cent_hbm.at[pl.ds(at, block)], cent.at[pl.ds(at, block)], t_sem.at[b]
        )

    emb_copy = pltpu.make_async_copy(emb_hbm, emb, e_sem)
    emb_copy.start()

    @pl.loop(0, NB)
    def _(t):
        cent_copy(block_at(t)).start()

    barrier = pltpu.get_barrier_semaphore()
    for peer in dp_peers:
        pl.semaphore_signal(barrier, inc=1, device_id={"dp": peer, "cent": c}, device_id_type=MESH)
    for peer in c_peers:
        pl.semaphore_signal(barrier, inc=1, device_id={"dp": d, "cent": peer}, device_id_type=MESH)

    emb_copy.wait()
    mine = pl.multiple_of(c * quarter, quarter)
    zb[z] = rms_rows(emb[pl.ds(mine, quarter), :]).astype(jnp.float32)
    pl.semaphore_wait(barrier, n_dp - 1 + n_cent - 1)

    low = z // 2
    first = z + 1 - 2 * low
    other = 2 * z - first
    last = 3 - 3 * low
    middle = (z == 1) | (z == 2)
    edge = jnp.logical_not(middle)
    near = jnp.where(middle, other, first)
    order = [near, last, 6 - z - near - last]
    n_items = 3 * PIECES

    def rows_of(p):
        return pl.ds(p * part_rows, part_rows)

    def z_copy(src, p, to, way, k):
        part = zb.at[src, rows_of(p)]
        return remote(part, part, z_send.at[way, k], z_recv.at[src, p], to * 2 + x, c)

    def z_arrival(i):
        j, p = divmod(i, PIECES)
        z_copy(order[j], p, first, 0, 0).wait_recv()

    def z_step(k):
        j, p = divmod(k, PIECES)
        if j == 0:

            @pl.when(edge)
            def _():
                z_copy(z, p, first, 0, k).start()

        @pl.when(middle)
        def _():
            if j == 1:
                z_arrival(k)
            z_copy(z if j == 0 else order[j], p, other, 1, k).start()
            if k < PIECES // 2:
                z_copy(z, p, first, 0, k).start()

    def z_between(i):
        if i < PIECES:

            @pl.when(middle)
            def _():
                z_copy(order[0], i, first, 0, PIECES + i).start()
        elif i < PIECES + PIECES // 2:
            p = i - PIECES // 2

            @pl.when(middle)
            def _():
                z_copy(z, p, first, 0, p).start()

    def z_drain():
        for p in range(PIECES):
            z_copy(z, p, first, 0, p).wait_send()

        @pl.when(middle)
        def _():
            for k in range(n_items):
                z_copy(z, k % PIECES, other, 1, k).wait_send()
            for p in range(PIECES):
                z_copy(z, p, first, 0, p + PIECES).wait_send()

    def x_copy(i):
        j, p = divmod(i, PIECES)
        return remote(
            zb.at[order[j], rows_of(p)], xg.at[order[j], c, rows_of(p)],
            x_send.at[i], x_recv.at[i], d_x, c,
        )

    def own_part(i, crossed):
        j, p = divmod(i, PIECES)
        return xg.at[order[j], c, rows_of(p)] if crossed else zb.at[order[j], rows_of(p)]

    def y_copy(i, crossed, who):
        j, p = divmod(i, PIECES)
        return remote(
            own_part(i, crossed), xg.at[order[j], who, rows_of(p)],
            y_send.at[i], y_recv.at[i], d, c_y,
        )

    def k_copy(i, crossed, who):
        j, p = divmod(i, PIECES)
        return remote(
            own_part(i, crossed), xg.at[order[j], who, rows_of(p)],
            k_send.at[i, 0], k_recv.at[i, 0], d, c_core,
        )

    def k_copy_y(i, who):
        j, p = divmod(i, PIECES)
        part = xg.at[order[j], who, rows_of(p)]
        return remote(part, part, k_send.at[i, 1], k_recv.at[i, 1], d, c_core)

    def spread(i, crossed):
        y_copy(i, crossed, c).start()
        k_copy(i, crossed, c).start()

    def crossing(j):
        return (None, edge, middle)[j], (None, middle, edge)[j]

    def stage_x(i):
        if i < PIECES:
            z_arrival(i)
            x_copy(i).start()
        else:

            @pl.when(crossing(i // PIECES)[0])
            def _():
                z_arrival(i)
                x_copy(i).start()

    def across(i):
        x_copy(i).wait()
        spread(i, True)

    def stage_y(i):
        if i < PIECES:
            across(i)
        else:

            @pl.when(edge)
            def _():
                across(i)

            @pl.when(middle)
            def _():
                spread(i, False)

    def stage_last(i):
        @pl.when(edge)
        def _():
            z_arrival(i)
            spread(i, False)

        @pl.when(middle)
        def _():
            across(i)

    def stage_core(i):
        y_copy(i, True, c_y).wait()
        k_copy_y(i, c_y).start()

    def stage_done(i):
        k_copy(i, True, c_core).wait()
        k_copy_y(i, c_core).wait()

    def step(plan):
        early = 2 * PIECES
        for k in plan[1]:
            if k < early:
                stage_x(k)
            elif k < n_items:
                stage_last(k)
            z_between(k)
            if early <= k + LAG_Y < n_items:
                stage_x(k + LAG_Y)
            if 0 <= k - LAG_Y < early:
                stage_y(k - LAG_Y)
            if 0 <= k - LAG_CORE < early:
                stage_core(k - LAG_CORE)
            if early <= k - LAG_Y < n_items:
                stage_core(k - LAG_Y)
        for k in plan[0]:
            z_step(k)

    def steps(where):
        step(PLAN[where])

    def steps_at(where, t):
        for at, plan in PLAN[where].items():

            @pl.when(t == at)
            def _():
                step(plan)

    def unpack(j):
        for p in range(PIECES):
            stage_done(j * PIECES + p)
        at = order[j] * rows
        for k in range(1, n_cent):
            who = lax.rem(c + k, n_cent)
            xb[pl.ds(pl.multiple_of(at + who * quarter, quarter), quarter), :] = xg[
                order[j], who
            ].astype(jnp.bfloat16)
        own = pl.ds(pl.multiple_of(at + c * quarter, quarter), quarter)
        if j == 0:
            xb[own, :] = xg[order[j], c].astype(jnp.bfloat16)
        else:
            crossed, straight = crossing(j)

            @pl.when(crossed)
            def _():
                xb[own, :] = xg[order[j], c].astype(jnp.bfloat16)

            @pl.when(straight)
            def _():
                xb[own, :] = zb[order[j]].astype(jnp.bfloat16)

    steps("start")
    base = pl.multiple_of(z * rows, rows)
    for i in range(n_cent):
        xb[pl.ds(base + i * quarter, quarter), :] = rms_rows(emb[i * quarter : (i + 1) * quarter, :])

    def c_copy(it, b, owner):
        return remote(co.at[it, b], cs.at[it, owner], c_send.at[it, b], c_recv.at[it, owner], b, c)

    def v_copy(it, owner, to):
        part = vb.at[it, owner]
        return remote(part, part, v_send.at[it, to], v_recv.at[it, owner], to, c)

    def r_copy(it, k, owner):
        part = rr.at[it, owner]
        return remote(part, part, r_send.at[it, k], r_recv.at[it, owner], d, c_peers[k])

    def column_part(it, t, b, col):
        row = jnp.sum(col, axis=0, keepdims=True)

        @pl.when(t == 0)
        def _():
            cs[it, d] = row

        @pl.when(t > 0)
        def _():
            co[it, b] = row
            c_copy(it, b, d).start()

    def exchange(it):
        rr[it, c] = to_row(racc[...])
        for k in range(n_cent - 1):
            r_copy(it, k, c).start()
        steps("sums%d" % it)
        for peer in dp_peers:
            c_copy(it, peer, peer).wait_recv()
        col_sum = cs[it, 0]
        for k in range(1, n_dp):
            col_sum = col_sum + cs[it, k]
        v_old = vb[it - 1, d] if it else jnp.ones((1, block), jnp.float32)
        vb[it, d] = jnp.sqrt(v_old * ratio / col_sum)
        if it < ITERS - 1:

            @pl.loop(1, NB)
            def _(t):
                v_copy(it, d, block_at(t)).start()
        else:
            v_copy(it, d, d_x).start()
            v_copy(it, d, d_z).start()
        steps("shared%d" % it)
        for k, peer in enumerate(c_peers):
            r_copy(it, k, peer).wait()
        row_sum = rr[it, 0]
        for k in range(1, n_cent):
            row_sum = row_sum + rr[it, k]
        u_old = uz[z] if it else jnp.ones((1, rows), jnp.float32)
        u_new = jnp.sqrt(u_old / row_sum)
        uz[z] = u_new
        if it < ITERS - 1:
            ucol[...] = to_column(u_new)

    racc[...] = jnp.zeros_like(racc)

    @pl.loop(0, NB)
    def _(t):
        steps_at("scores", t)
        b = block_at(t)
        at = pl.multiple_of(b * block, block)
        cent_copy(b).wait()
        ch_b = rms_rows(cent[pl.ds(at, block), :])
        ch[pl.ds(at, block), :] = ch_b
        col = jnp.zeros((8, block), jnp.float32)
        for i in range(n_cent):
            part = slice(i * quarter, (i + 1) * quarter)
            s = lax.dot_general(
                xb[pl.ds(base + i * quarter, quarter), :], ch_b, NT,
                preferred_element_type=jnp.float32,
            )
            e = jnp.exp(s * scale)
            energy[b, part, :] = e
            racc[part, :] += lane_tiles(e)
            col = col + jnp.sum(e.reshape(quarter // 8, 8, block), axis=0)
        column_part(0, t, b, col)

    exchange(0)

    group = 64
    for it in range(1, ITERS):
        racc[...] = jnp.zeros_like(racc)

        @pl.loop(0, NB)
        def _(t):
            steps_at("pass%d" % it, t)
            b = block_at(t)

            @pl.when(t > 0)
            def _():
                v_copy(it - 1, b, d_x).wait_recv()

            v_b = jnp.broadcast_to(vb[it - 1, b], (8, block))

            def rows_step(g, col):
                r0 = pl.multiple_of(g * group, group)
                for i in range(group // 8):
                    e = energy[b, pl.ds(r0 + i * 8, 8), :]
                    u8 = ucol[pl.ds(r0 + i * 8, 8), :]
                    col = col + e * jnp.concatenate([u8] * (block // 128), axis=1)
                    racc[pl.ds(r0 + i * 8, 8), :] += lane_tiles(e * v_b)
                return col

            col = lax.fori_loop(0, rows // group, rows_step, jnp.zeros((8, block), jnp.float32))
            column_part(it, t, b, col)

        exchange(it)

    def u_copy(k, owner):
        to = lax.rem(z + k, n_z)
        return remote(
            uz.at[owner], uz.at[owner], u_send.at[k - 1], u_recv.at[owner],
            to * 2 + lax.rem(x + k, 2), c,
        )

    for k in range(1, n_z):
        u_copy(k, z).start()
    final = ITERS - 1
    owners = (d_x, d_z, d, d)

    def column_scales(qs):
        for q in qs:
            s = q % 2
            vcol[q] = to_column(vb[final, owners[q]][:, s * CHUNK : (s + 1) * CHUNK])

    column_scales((2, 3))
    wacc[...] = jnp.zeros_like(wacc)
    cacc[...] = jnp.zeros_like(cacc)
    steps("u")

    def weigh(q, blocks):
        owner = jnp.where(q == 0, d_x, jnp.where(q == 1, d_z, d))
        at = pl.multiple_of(owner * block + lax.rem(q, 2) * CHUNK, CHUNK)
        cc = ch[pl.ds(at, CHUNK), :]
        v_tile = jnp.concatenate([vcol[q]] * (block // 128), axis=1)
        for first_row, u in blocks:
            xr = xb[pl.ds(pl.multiple_of(first_row, block), block), :]
            e = jnp.exp(lax.dot_general(cc, xr, NT, preferred_element_type=jnp.float32) * scale)
            cacc[q] += lane_tiles(e * u)
            w = ((total_cents * u) * e * v_tile).astype(jnp.bfloat16)
            wacc[q] += jnp.dot(w, xr, preferred_element_type=jnp.float32)

    def whole(src):
        return [
            (src * rows + h * block, uz[src][:, h * block : (h + 1) * block])
            for h in range(rows // block)
        ]

    n_out = 2 * (n_z - 1)

    def unit(t):
        late = jnp.maximum(t - n_out, 0)
        j = jnp.where(t < n_out, t, late) // 2
        src = jnp.where(j == 0, z, jnp.where(j == 1, order[0], jnp.where(j == 2, order[1], order[2])))
        weigh(lax.rem(t, 2) + jnp.where(t < n_out, 0, 2), whole(src))

    @pl.loop(0, n_out + AHEAD)
    def _(t):
        steps_at("weigh", t)

        @pl.when(t == 0)
        def _():
            v_copy(final, d_x, d_x).wait_recv()
            v_copy(final, d_z, d_z).wait_recv()
            column_scales((0, 1))

        @pl.when(t == 2)
        def _():
            unpack(0)
            for k in range(1, n_z):
                u_copy(k, lax.rem(z + k, n_z)).wait()

        @pl.when(t == 4)
        def _():
            unpack(1)

        unit(t)

    unpack(2)

    def w_copy(s):
        return remote(wacc.at[s], wr.at[s], w_send.at[s], w_recv.at[s], owners[s], c)

    def f_copy(s):
        return remote(cfs.at[s], cfr.at[s], w_send.at[2 + s], w_recv.at[2 + s], owners[s], c)

    @pl.loop(0, 2)
    def _(q):
        weigh(q, whole(order[2]))
        cfs[q] = to_row(cacc[q])
        for s in range(2):

            @pl.when(q == s)
            def _():
                w_copy(s).start()
                f_copy(s).start()

    @pl.loop(n_out + AHEAD, n_out + 2 * n_z)
    def _(t):
        unit(t)

    for q in (2, 3):
        cfs[q] = to_row(cacc[q])
    z_drain()
    for it in range(ITERS):

        @pl.loop(1, NB)
        def _(t):
            b = block_at(t)
            c_copy(it, b, d).wait_send()
            if it < final:
                v_copy(it, d, b).wait_send()

    v_copy(final, d, d_x).wait_send()
    v_copy(final, d, d_z).wait_send()
    for s in range(2):
        f_copy(s).wait()
        w_copy(s).wait()
        w = wacc[2 + s] + wr[s]
        out_w[s] = w * lax.rsqrt(jnp.mean(w * w, axis=1, keepdims=True) + 1e-06)
        half = slice(s * CHUNK, (s + 1) * CHUNK)
        out_m[:, half] = (
            vb[final, d][:, half] * (cfs[2 + s] + cfr[s]) * (total_cents / total_rows)
        )


def fused(embeddings, centroids):
    n_dp, n_cent = lax.axis_size("dp"), lax.axis_size("cent")
    rows, width = embeddings.shape
    cents = centroids.shape[0]
    n_z = n_dp // 2
    block = cents // NB
    quarter = rows // n_cent
    n_s = block // CHUNK
    n_items = 3 * PIECES
    f32 = jnp.float32
    dma = pltpu.SemaphoreType.DMA
    w, m = pl.pallas_call(
        functools.partial(
            kernel, float(rows * n_dp), float(cents * n_cent), n_dp, n_cent
        ),
        out_shape=(
            pltpu.VMEM((n_s, CHUNK, width), f32),
            pltpu.VMEM((1, block), f32),
        ),
        in_specs=[pl.BlockSpec(memory_space=pl.ANY)] * 2,
        out_specs=(pl.BlockSpec(memory_space=pltpu.VMEM),) * 2,
        scratch_shapes=[
            pltpu.VMEM((rows, width), jnp.bfloat16),
            pltpu.VMEM((cents, width), jnp.bfloat16),
            pltpu.VMEM((NB, rows, block), f32),
            pltpu.VMEM((cents, width), jnp.bfloat16),
            pltpu.VMEM((n_z, quarter, width), f32),
            pltpu.VMEM((n_z, n_cent, quarter, width), f32),
            pltpu.VMEM((n_z * rows, width), jnp.bfloat16),
            pltpu.VMEM((rows, 128), f32),
            pltpu.VMEM((rows, 128), f32),
            pltpu.VMEM((ITERS, NB, 1, block), f32),
            pltpu.VMEM((ITERS, n_dp, 1, block), f32),
            pltpu.VMEM((ITERS, n_dp, 1, block), f32),
            pltpu.VMEM((2 * n_s, CHUNK, 128), f32),
            pltpu.VMEM((ITERS, n_cent, 1, rows), f32),
            pltpu.VMEM((n_z, 1, rows), f32),
            pltpu.VMEM((2 * n_s, CHUNK, width), f32),
            pltpu.VMEM((n_s, CHUNK, width), f32),
            pltpu.VMEM((2 * n_s, CHUNK, 128), f32),
            pltpu.VMEM((2 * n_s, 1, CHUNK), f32),
            pltpu.VMEM((n_s, 1, CHUNK), f32),
            dma,
            dma((NB,)),
            dma((ITERS, n_dp)),
            dma((ITERS, n_dp)),
            dma((ITERS, n_dp)),
            dma((ITERS, n_dp)),
            dma((ITERS, n_cent - 1)),
            dma((ITERS, n_cent)),
            dma((2, n_items)),
            dma((n_z, PIECES)),
            dma((n_items,)),
            dma((n_items,)),
            dma((n_items,)),
            dma((n_items,)),
            dma((n_items, 2)),
            dma((n_items, 2)),
            dma((n_z - 1,)),
            dma((n_z,)),
            dma((2 * n_s,)),
            dma((2 * n_s,)),
        ],
        compiler_params=pltpu.CompilerParams(
            collective_id=0, has_side_effects=True, vmem_limit_bytes=60 * 2**20
        ),
    )(embeddings, centroids)
    return w.reshape(block, width), m.reshape(block)


def column_total(weights, energy):
    return lax.psum(jnp.dot(weights, energy, precision=lax.Precision.HIGHEST), "dp")


def local(embeddings, centroids):
    n_data = lax.axis_size("dp")
    xh = rms_rows(embeddings)
    ch = rms_rows(centroids)
    local_rows, width = xh.shape
    local_cents = ch.shape[0]
    total_rows = float(local_rows * n_data)
    total_cents = float(local_cents * lax.axis_size("cent"))
    scores = lax.dot_general(xh, ch, NT, preferred_element_type=jnp.float32)
    energy = jnp.exp(scores * (1.0 / (TAU * width)))
    u = jnp.ones((local_rows,), jnp.float32)
    v = jnp.ones((local_cents,), jnp.float32)
    for step_index in range(ITERS):
        rows_sum = lax.psum(jnp.dot(energy, v, precision=lax.Precision.HIGHEST), "cent")
        cols = column_total(u, energy)
        u, v = (jnp.sqrt(u / rows_sum), jnp.sqrt(v * (total_rows / total_cents) / cols))
    cols = column_total(u, energy)
    plan = (total_cents * u[:, None] * energy * v[None, :]).astype(jnp.bfloat16)
    share = local_cents // n_data
    weighted = lax.dot_general(
        plan, xh, (((0,), (0,)), ((), ())), preferred_element_type=jnp.float32
    )
    mine = lax.psum_scatter(weighted, "dp", scatter_dimension=0, tiled=True)
    mass_all = v * cols * (total_cents / total_rows)
    column_mass = lax.dynamic_slice_in_dim(mass_all, lax.axis_index("dp") * share, share, 0)
    new_centroids = mine * lax.rsqrt(jnp.mean(mine * mine, axis=1, keepdims=True) + 1e-06)
    return (new_centroids, column_mass)


def solution(mesh):
    in_specs = (P("dp", None), P("cent", None))
    out_specs = (P(("cent", "dp"), None), P(("cent", "dp")))
    small = mesh.shape["dp"] == NB and mesh.shape["cent"] == 4
    body = fused if small else local
    return jax.shard_map(body, mesh=mesh, in_specs=in_specs, out_specs=out_specs, check_vma=False)
```

```python
import functools
import jax
import jax.numpy as jnp
from jax import lax
from jax.experimental import pallas as pl
from jax.experimental.pallas import tpu as pltpu
from jax.sharding import PartitionSpec as P

ITERS = 3
TAU = 0.02
MESH = pl.DeviceIdType.MESH
NT = (((1,), (1,)), ((), ()))
NB = 8
CHUNK = 256
PIECES = 8
LAG_Y, LAG_CORE = 3, 6
AHEAD = 0
PLAN = {
    "start": ((0, 1, 2, 3, 4, 5), ()),
    "scores": {3: ((), (0,)), 4: ((), (1,)), 5: ((6,), (2,)), 6: ((), (3,)), 7: ((7,), (4,))},
    "sums0": ((8,), (5,)),
    "shared0": ((9, 10), (6, 7)),
    "pass1": {0: ((11,), (8,)), 2: ((12,), (9,)), 3: ((), (10,)), 5: ((13,), (11,))},
    "sums1": ((14,), (12,)),
    "shared1": ((15, 16), (13, 14)),
    "pass2": {0: ((17,), (15,)), 2: ((18,), (16,)), 4: ((19,), (17,))},
    "sums2": ((20,), (18,)),
    "shared2": ((21, 22), (19, 20)),
    "u": ((23,), (21,)),
    "weigh": {0: ((), (22, 23)), 1: ((), (24,)), 2: ((), (25,)), 3: ((), (26,))},
}


def rms_rows(values):
    wide = values.astype(jnp.float32)
    return (wide * lax.rsqrt(jnp.mean(wide * wide, axis=1, keepdims=True) + 1e-06)).astype(
        jnp.bfloat16
    )


def lane_tiles(values):
    total = values[:, :128]
    for t in range(1, values.shape[1] // 128):
        total = total + values[:, t * 128 : (t + 1) * 128]
    return total


def to_column(row):
    return jnp.broadcast_to(row, (128, row.shape[1])).T


def to_row(tile):
    return jnp.sum(tile.T, axis=0, keepdims=True)


def kernel(
    total_rows, total_cents, n_dp, n_cent,
    emb_hbm, cent_hbm, out_w, out_m,
    emb, cent, energy, ch, zb, xg, xb, ucol, racc, co, cs, vb, vcol, rr, uz, wacc, wr, cacc, cfs, cfr,
    e_sem, t_sem, c_send, c_recv, v_send, v_recv, r_send, r_recv,
    z_send, z_recv, x_send, x_recv, y_send, y_recv, k_send, k_recv,
    u_send, u_recv, w_send, w_recv,
):
    n_z = n_dp // 2
    rows, width = emb.shape
    cents = cent.shape[0]
    block = cents // NB
    quarter = rows // n_cent
    part_rows = quarter // PIECES
    scale = 1.0 / (TAU * width)
    ratio = total_rows / total_cents
    d = lax.axis_index("dp")
    c = lax.axis_index("cent")
    z, x = d // 2, lax.rem(d, 2)
    y, core = c // 2, lax.rem(c, 2)
    dp_peers = [lax.rem(d + k, n_dp) for k in range(1, n_dp)]
    c_peers = [lax.rem(c + k, n_cent) for k in range(1, n_cent)]
    c_y = (1 - y) * 2 + core
    c_core = y * 2 + (1 - core)
    d_x = z * 2 + (1 - x)
    z_pair = z + 1 - 2 * lax.rem(z, 2)
    d_z = z_pair * 2 + x

    def block_at(t):
        pair = t // 2
        at_z = jnp.where(
            pair == 0, z, jnp.where(pair == 1, lax.rem(z + 2, n_z), jnp.where(pair == 2, 3 - z, z_pair))
        )
        return at_z * 2 + lax.rem(x + t + t // 6, 2)

    def remote(src, dst, ssem, rsem, dp, cn):
        return pltpu.make_async_remote_copy(
            src_ref=src, dst_ref=dst, send_sem=ssem, recv_sem=rsem,
            device_id={"dp": dp, "cent": cn}, device_id_type=MESH,
        )

    def cent_copy(b):
        at = pl.multiple_of(b * block, block)
        return pltpu.make_async_copy(
            cent_hbm.at[pl.ds(at, block)], cent.at[pl.ds(at, block)], t_sem.at[b]
        )

    emb_copy = pltpu.make_async_copy(emb_hbm, emb, e_sem)
    emb_copy.start()

    @pl.loop(0, NB)
    def _(t):
        cent_copy(block_at(t)).start()

    barrier = pltpu.get_barrier_semaphore()
    for peer in dp_peers:
        pl.semaphore_signal(barrier, inc=1, device_id={"dp": peer, "cent": c}, device_id_type=MESH)
    for peer in c_peers:
        pl.semaphore_signal(barrier, inc=1, device_id={"dp": d, "cent": peer}, device_id_type=MESH)

    emb_copy.wait()
    mine = pl.multiple_of(c * quarter, quarter)
    zb[z] = rms_rows(emb[pl.ds(mine, quarter), :]).astype(jnp.float32)
    pl.semaphore_wait(barrier, n_dp - 1 + n_cent - 1)

    low = z // 2
    first = z + 1 - 2 * low
    other = 2 * z - first
    last = 3 - 3 * low
    middle = (z == 1) | (z == 2)
    edge = jnp.logical_not(middle)
    near = jnp.where(middle, other, first)
    order = [near, last, 6 - z - near - last]
    n_items = 3 * PIECES

    def rows_of(p):
        return pl.ds(p * part_rows, part_rows)

    def z_copy(src, p, to, way, k):
        part = zb.at[src, rows_of(p)]
        return remote(part, part, z_send.at[way, k], z_recv.at[src, p], to * 2 + x, c)

    def z_arrival(i):
        j, p = divmod(i, PIECES)
        z_copy(order[j], p, first, 0, 0).wait_recv()

    def z_step(k):
        j, p = divmod(k, PIECES)
        if j == 0:

            @pl.when(edge)
            def _():
                z_copy(z, p, first, 0, k).start()

        @pl.when(middle)
        def _():
            if j == 1:
                z_arrival(k)
            z_copy(z if j == 0 else order[j], p, other, 1, k).start()
            if k < PIECES // 2:
                z_copy(z, p, first, 0, k).start()

    def z_between(i):
        if i < PIECES:

            @pl.when(middle)
            def _():
                z_copy(order[0], i, first, 0, PIECES + i).start()
        elif i < PIECES + PIECES // 2:
            p = i - PIECES // 2

            @pl.when(middle)
            def _():
                z_copy(z, p, first, 0, p).start()

    def z_drain():
        for p in range(PIECES):
            z_copy(z, p, first, 0, p).wait_send()

        @pl.when(middle)
        def _():
            for k in range(n_items):
                z_copy(z, k % PIECES, other, 1, k).wait_send()
            for p in range(PIECES):
                z_copy(z, p, first, 0, p + PIECES).wait_send()

    def x_copy(i):
        j, p = divmod(i, PIECES)
        return remote(
            zb.at[order[j], rows_of(p)], xg.at[order[j], c, rows_of(p)],
            x_send.at[i], x_recv.at[i], d_x, c,
        )

    def own_part(i, crossed):
        j, p = divmod(i, PIECES)
        return xg.at[order[j], c, rows_of(p)] if crossed else zb.at[order[j], rows_of(p)]

    def y_copy(i, crossed, who):
        j, p = divmod(i, PIECES)
        return remote(
            own_part(i, crossed), xg.at[order[j], who, rows_of(p)],
            y_send.at[i], y_recv.at[i], d, c_y,
        )

    def k_copy(i, crossed, who):
        j, p = divmod(i, PIECES)
        return remote(
            own_part(i, crossed), xg.at[order[j], who, rows_of(p)],
            k_send.at[i, 0], k_recv.at[i, 0], d, c_core,
        )

    def k_copy_y(i, who):
        j, p = divmod(i, PIECES)
        part = xg.at[order[j], who, rows_of(p)]
        return remote(part, part, k_send.at[i, 1], k_recv.at[i, 1], d, c_core)

    def spread(i, crossed):
        y_copy(i, crossed, c).start()
        k_copy(i, crossed, c).start()

    def crossing(j):
        return (None, edge, middle)[j], (None, middle, edge)[j]

    def stage_x(i):
        if i < PIECES:
            z_arrival(i)
            x_copy(i).start()
        else:

            @pl.when(crossing(i // PIECES)[0])
            def _():
                z_arrival(i)
                x_copy(i).start()

    def across(i):
        x_copy(i).wait()
        spread(i, True)

    def stage_y(i):
        if i < PIECES:
            across(i)
        else:

            @pl.when(edge)
            def _():
                across(i)

            @pl.when(middle)
            def _():
                spread(i, False)

    def stage_last(i):
        @pl.when(edge)
        def _():
            z_arrival(i)
            spread(i, False)

        @pl.when(middle)
        def _():
            across(i)

    def stage_core(i):
        y_copy(i, True, c_y).wait()
        k_copy_y(i, c_y).start()

    def stage_done(i):
        k_copy(i, True, c_core).wait()
        k_copy_y(i, c_core).wait()

    def step(plan):
        early = 2 * PIECES
        for k in plan[1]:
            if k < early:
                stage_x(k)
            elif k < n_items:
                stage_last(k)
            z_between(k)
            if early <= k + LAG_Y < n_items:
                stage_x(k + LAG_Y)
            if 0 <= k - LAG_Y < early:
                stage_y(k - LAG_Y)
            if 0 <= k - LAG_CORE < early:
                stage_core(k - LAG_CORE)
            if early <= k - LAG_Y < n_items:
                stage_core(k - LAG_Y)
        for k in plan[0]:
            z_step(k)

    def steps(where):
        step(PLAN[where])

    def steps_at(where, t):
        for at, plan in PLAN[where].items():

            @pl.when(t == at)
            def _():
                step(plan)

    def unpack(j):
        for p in range(PIECES):
            stage_done(j * PIECES + p)
        at = order[j] * rows
        for k in range(1, n_cent):
            who = lax.rem(c + k, n_cent)
            xb[pl.ds(pl.multiple_of(at + who * quarter, quarter), quarter), :] = xg[
                order[j], who
            ].astype(jnp.bfloat16)
        own = pl.ds(pl.multiple_of(at + c * quarter, quarter), quarter)
        if j == 0:
            xb[own, :] = xg[order[j], c].astype(jnp.bfloat16)
        else:
            crossed, straight = crossing(j)

            @pl.when(crossed)
            def _():
                xb[own, :] = xg[order[j], c].astype(jnp.bfloat16)

            @pl.when(straight)
            def _():
                xb[own, :] = zb[order[j]].astype(jnp.bfloat16)

    steps("start")
    base = pl.multiple_of(z * rows, rows)
    for i in range(n_cent):
        xb[pl.ds(base + i * quarter, quarter), :] = rms_rows(emb[i * quarter : (i + 1) * quarter, :])

    def c_copy(it, b, owner):
        return remote(co.at[it, b], cs.at[it, owner], c_send.at[it, b], c_recv.at[it, owner], b, c)

    def v_copy(it, owner, to):
        part = vb.at[it, owner]
        return remote(part, part, v_send.at[it, to], v_recv.at[it, owner], to, c)

    def r_copy(it, k, owner):
        part = rr.at[it, owner]
        return remote(part, part, r_send.at[it, k], r_recv.at[it, owner], d, c_peers[k])

    def column_part(it, t, b, col):
        row = jnp.sum(col, axis=0, keepdims=True)

        @pl.when(t == 0)
        def _():
            cs[it, d] = row

        @pl.when(t > 0)
        def _():
            co[it, b] = row
            c_copy(it, b, d).start()

    def exchange(it):
        rr[it, c] = to_row(racc[...])
        for k in range(n_cent - 1):
            r_copy(it, k, c).start()
        steps("sums%d" % it)
        for peer in dp_peers:
            c_copy(it, peer, peer).wait_recv()
        col_sum = cs[it, 0]
        for k in range(1, n_dp):
            col_sum = col_sum + cs[it, k]
        v_old = vb[it - 1, d] if it else jnp.ones((1, block), jnp.float32)
        vb[it, d] = jnp.sqrt(v_old * ratio / col_sum)
        if it < ITERS - 1:

            @pl.loop(1, NB)
            def _(t):
                v_copy(it, d, block_at(t)).start()
        else:
            v_copy(it, d, d_x).start()
            v_copy(it, d, d_z).start()
        steps("shared%d" % it)
        for k, peer in enumerate(c_peers):
            r_copy(it, k, peer).wait()
        row_sum = rr[it, 0]
        for k in range(1, n_cent):
            row_sum = row_sum + rr[it, k]
        u_old = uz[z] if it else jnp.ones((1, rows), jnp.float32)
        u_new = jnp.sqrt(u_old / row_sum)
        uz[z] = u_new
        if it < ITERS - 1:
            ucol[...] = to_column(u_new)

    racc[...] = jnp.zeros_like(racc)

    @pl.loop(0, NB)
    def _(t):
        steps_at("scores", t)
        b = block_at(t)
        at = pl.multiple_of(b * block, block)
        cent_copy(b).wait()
        ch_b = rms_rows(cent[pl.ds(at, block), :])
        ch[pl.ds(at, block), :] = ch_b
        col = jnp.zeros((8, block), jnp.float32)
        for i in range(n_cent):
            part = slice(i * quarter, (i + 1) * quarter)
            s = lax.dot_general(
                xb[pl.ds(base + i * quarter, quarter), :], ch_b, NT,
                preferred_element_type=jnp.float32,
            )
            e = jnp.exp(s * scale)
            energy[b, part, :] = e
            racc[part, :] += lane_tiles(e)
            col = col + jnp.sum(e.reshape(quarter // 8, 8, block), axis=0)
        column_part(0, t, b, col)

    exchange(0)

    group = 64
    for it in range(1, ITERS):
        racc[...] = jnp.zeros_like(racc)

        @pl.loop(0, NB)
        def _(t):
            steps_at("pass%d" % it, t)
            b = block_at(t)

            @pl.when(t > 0)
            def _():
                v_copy(it - 1, b, d_x).wait_recv()

            v_b = jnp.broadcast_to(vb[it - 1, b], (8, block))

            def rows_step(g, col):
                r0 = pl.multiple_of(g * group, group)
                for i in range(group // 8):
                    e = energy[b, pl.ds(r0 + i * 8, 8), :]
                    u8 = ucol[pl.ds(r0 + i * 8, 8), :]
                    col = col + e * jnp.concatenate([u8] * (block // 128), axis=1)
                    racc[pl.ds(r0 + i * 8, 8), :] += lane_tiles(e * v_b)
                return col

            col = lax.fori_loop(0, rows // group, rows_step, jnp.zeros((8, block), jnp.float32))
            column_part(it, t, b, col)

        exchange(it)

    def u_copy(k, owner):
        to = lax.rem(z + k, n_z)
        return remote(
            uz.at[owner], uz.at[owner], u_send.at[k - 1], u_recv.at[owner],
            to * 2 + lax.rem(x + k, 2), c,
        )

    for k in range(1, n_z):
        u_copy(k, z).start()
    final = ITERS - 1
    owners = (d_x, d_z, d, d)

    def column_scales(qs):
        for q in qs:
            s = q % 2
            vcol[q] = to_column(vb[final, owners[q]][:, s * CHUNK : (s + 1) * CHUNK])

    column_scales((2, 3))
    wacc[...] = jnp.zeros_like(wacc)
    cacc[...] = jnp.zeros_like(cacc)
    steps("u")

    def weigh(q, blocks, start=0, count=CHUNK):
        part = pl.ds(start, count)
        owner = jnp.where(q == 0, d_x, jnp.where(q == 1, d_z, d))
        at = pl.multiple_of(owner * block + lax.rem(q, 2) * CHUNK + start, count)
        cc = ch[pl.ds(at, count), :]
        v_tile = jnp.concatenate([vcol[q, part]] * (block // 128), axis=1)
        for first_row, u in blocks:
            xr = xb[pl.ds(pl.multiple_of(first_row, block), block), :]
            e = jnp.exp(lax.dot_general(cc, xr, NT, preferred_element_type=jnp.float32) * scale)
            cacc[q, part] += lane_tiles(e * u)
            w = ((total_cents * u) * e * v_tile).astype(jnp.bfloat16)
            wacc[q, part] += jnp.dot(w, xr, preferred_element_type=jnp.float32)

    def whole(src):
        return [
            (src * rows + h * block, uz[src][:, h * block : (h + 1) * block])
            for h in range(rows // block)
        ]

    n_out = 2 * (n_z - 1)

    def unit(t):
        late = jnp.maximum(t - n_out, 0)
        j = jnp.where(t < n_out, t, late) // 2
        src = jnp.where(j == 0, z, jnp.where(j == 1, order[0], jnp.where(j == 2, order[1], order[2])))
        weigh(lax.rem(t, 2) + jnp.where(t < n_out, 0, 2), whole(src))

    @pl.loop(0, n_out + AHEAD)
    def _(t):
        steps_at("weigh", t)

        @pl.when(t == 0)
        def _():
            v_copy(final, d_x, d_x).wait_recv()
            v_copy(final, d_z, d_z).wait_recv()
            column_scales((0, 1))

        @pl.when(t == 2)
        def _():
            unpack(0)
            for k in range(1, n_z):
                u_copy(k, lax.rem(z + k, n_z)).wait()

        @pl.when(t == 4)
        def _():
            unpack(1)

        unit(t)

    unpack(2)

    half = CHUNK // 2

    def w_copy(s, h):
        part = pl.ds(h * half, half)
        return remote(
            wacc.at[s, part], wr.at[s, part], w_send.at[2 * h + s], w_recv.at[2 * h + s],
            owners[s], c,
        )

    def f_copy(s):
        return remote(cfs.at[s], cfr.at[s], w_send.at[4 + s], w_recv.at[4 + s], owners[s], c)

    @pl.loop(0, 4)
    def _(t):
        weigh(lax.rem(t, 2), whole(order[2]), pl.multiple_of((t // 2) * half, half), half)
        for h in range(2):
            for s in range(2):

                @pl.when(t == 2 * h + s)
                def _():
                    w_copy(s, h).start()

    for s in range(2):
        cfs[s] = to_row(cacc[s])
        f_copy(s).start()

    @pl.loop(n_out + AHEAD, n_out + 2 * n_z)
    def _(t):
        unit(t)

    for q in (2, 3):
        cfs[q] = to_row(cacc[q])
    z_drain()
    for it in range(ITERS):

        @pl.loop(1, NB)
        def _(t):
            b = block_at(t)
            c_copy(it, b, d).wait_send()
            if it < final:
                v_copy(it, d, b).wait_send()

    v_copy(final, d, d_x).wait_send()
    v_copy(final, d, d_z).wait_send()
    for h in range(2):
        part = slice(h * half, (h + 1) * half)
        for s in range(2):
            w_copy(s, h).wait()
            w = wacc[2 + s, part] + wr[s, part]
            out_w[s, part] = w * lax.rsqrt(jnp.mean(w * w, axis=1, keepdims=True) + 1e-06)
    for s in range(2):
        f_copy(s).wait()
        lanes = slice(s * CHUNK, (s + 1) * CHUNK)
        out_m[:, lanes] = (
            vb[final, d][:, lanes] * (cfs[2 + s] + cfr[s]) * (total_cents / total_rows)
        )


def fused(embeddings, centroids):
    n_dp, n_cent = lax.axis_size("dp"), lax.axis_size("cent")
    rows, width = embeddings.shape
    cents = centroids.shape[0]
    n_z = n_dp // 2
    block = cents // NB
    quarter = rows // n_cent
    n_s = block // CHUNK
    n_items = 3 * PIECES
    f32 = jnp.float32
    dma = pltpu.SemaphoreType.DMA
    w, m = pl.pallas_call(
        functools.partial(
            kernel, float(rows * n_dp), float(cents * n_cent), n_dp, n_cent
        ),
        out_shape=(
            pltpu.VMEM((n_s, CHUNK, width), f32),
            pltpu.VMEM((1, block), f32),
        ),
        in_specs=[pl.BlockSpec(memory_space=pl.ANY)] * 2,
        out_specs=(pl.BlockSpec(memory_space=pltpu.VMEM),) * 2,
        scratch_shapes=[
            pltpu.VMEM((rows, width), jnp.bfloat16),
            pltpu.VMEM((cents, width), jnp.bfloat16),
            pltpu.VMEM((NB, rows, block), f32),
            pltpu.VMEM((cents, width), jnp.bfloat16),
            pltpu.VMEM((n_z, quarter, width), f32),
            pltpu.VMEM((n_z, n_cent, quarter, width), f32),
            pltpu.VMEM((n_z * rows, width), jnp.bfloat16),
            pltpu.VMEM((rows, 128), f32),
            pltpu.VMEM((rows, 128), f32),
            pltpu.VMEM((ITERS, NB, 1, block), f32),
            pltpu.VMEM((ITERS, n_dp, 1, block), f32),
            pltpu.VMEM((ITERS, n_dp, 1, block), f32),
            pltpu.VMEM((2 * n_s, CHUNK, 128), f32),
            pltpu.VMEM((ITERS, n_cent, 1, rows), f32),
            pltpu.VMEM((n_z, 1, rows), f32),
            pltpu.VMEM((2 * n_s, CHUNK, width), f32),
            pltpu.VMEM((n_s, CHUNK, width), f32),
            pltpu.VMEM((2 * n_s, CHUNK, 128), f32),
            pltpu.VMEM((2 * n_s, 1, CHUNK), f32),
            pltpu.VMEM((n_s, 1, CHUNK), f32),
            dma,
            dma((NB,)),
            dma((ITERS, n_dp)),
            dma((ITERS, n_dp)),
            dma((ITERS, n_dp)),
            dma((ITERS, n_dp)),
            dma((ITERS, n_cent - 1)),
            dma((ITERS, n_cent)),
            dma((2, n_items)),
            dma((n_z, PIECES)),
            dma((n_items,)),
            dma((n_items,)),
            dma((n_items,)),
            dma((n_items,)),
            dma((n_items, 2)),
            dma((n_items, 2)),
            dma((n_z - 1,)),
            dma((n_z,)),
            dma((3 * n_s,)),
            dma((3 * n_s,)),
        ],
        compiler_params=pltpu.CompilerParams(
            collective_id=0, has_side_effects=True, vmem_limit_bytes=60 * 2**20
        ),
    )(embeddings, centroids)
    return w.reshape(block, width), m.reshape(block)


def column_total(weights, energy):
    return lax.psum(jnp.dot(weights, energy, precision=lax.Precision.HIGHEST), "dp")


def local(embeddings, centroids):
    n_data = lax.axis_size("dp")
    xh = rms_rows(embeddings)
    ch = rms_rows(centroids)
    local_rows, width = xh.shape
    local_cents = ch.shape[0]
    total_rows = float(local_rows * n_data)
    total_cents = float(local_cents * lax.axis_size("cent"))
    scores = lax.dot_general(xh, ch, NT, preferred_element_type=jnp.float32)
    energy = jnp.exp(scores * (1.0 / (TAU * width)))
    u = jnp.ones((local_rows,), jnp.float32)
    v = jnp.ones((local_cents,), jnp.float32)
    for step_index in range(ITERS):
        rows_sum = lax.psum(jnp.dot(energy, v, precision=lax.Precision.HIGHEST), "cent")
        cols = column_total(u, energy)
        u, v = (jnp.sqrt(u / rows_sum), jnp.sqrt(v * (total_rows / total_cents) / cols))
    cols = column_total(u, energy)
    plan = (total_cents * u[:, None] * energy * v[None, :]).astype(jnp.bfloat16)
    share = local_cents // n_data
    weighted = lax.dot_general(
        plan, xh, (((0,), (0,)), ((), ())), preferred_element_type=jnp.float32
    )
    mine = lax.psum_scatter(weighted, "dp", scatter_dimension=0, tiled=True)
    mass_all = v * cols * (total_cents / total_rows)
    column_mass = lax.dynamic_slice_in_dim(mass_all, lax.axis_index("dp") * share, share, 0)
    new_centroids = mine * lax.rsqrt(jnp.mean(mine * mine, axis=1, keepdims=True) + 1e-06)
    return (new_centroids, column_mass)


def solution(mesh):
    in_specs = (P("dp", None), P("cent", None))
    out_specs = (P(("cent", "dp"), None), P(("cent", "dp")))
    small = mesh.shape["dp"] == NB and mesh.shape["cent"] == 4
    body = fused if small else local
    return jax.shard_map(body, mesh=mesh, in_specs=in_specs, out_specs=out_specs, check_vma=False)
```

```python
import functools
import jax
import jax.numpy as jnp
from jax import lax
from jax.experimental import pallas as pl
from jax.experimental.pallas import tpu as pltpu
from jax.sharding import PartitionSpec as P

ITERS = 3
TAU = 0.02
MESH = pl.DeviceIdType.MESH
NT = (((1,), (1,)), ((), ()))
NB = 8
CHUNK = 256
PIECES = 8
LAG_Y, LAG_CORE = 3, 6
AHEAD = 0
PLAN = {
    "start": ((0, 1, 2, 3, 4, 5), ()),
    "scores": {3: ((), (0,)), 4: ((), (1,)), 5: ((6,), (2,)), 6: ((), (3,)), 7: ((7,), (4,))},
    "sums0": ((8,), (5,)),
    "shared0": ((9, 10), (6, 7)),
    "pass1": {0: ((11,), (8,)), 2: ((12,), (9,)), 3: ((), (10,)), 5: ((13,), (11,))},
    "sums1": ((14,), (12,)),
    "shared1": ((15, 16), (13, 14)),
    "pass2": {0: ((17,), (15,)), 2: ((18,), (16,)), 4: ((19,), (17,))},
    "sums2": ((20,), (18,)),
    "shared2": ((21, 22), (19, 20)),
    "u": ((23,), (21,)),
    "weigh": {0: ((), (22, 23)), 1: ((), (24,)), 2: ((), (25,)), 3: ((), (26,))},
}


def rms_rows(values):
    wide = values.astype(jnp.float32)
    return (wide * lax.rsqrt(jnp.mean(wide * wide, axis=1, keepdims=True) + 1e-06)).astype(
        jnp.bfloat16
    )


def lane_tiles(values):
    total = values[:, :128]
    for t in range(1, values.shape[1] // 128):
        total = total + values[:, t * 128 : (t + 1) * 128]
    return total


def to_column(row):
    return jnp.broadcast_to(row, (128, row.shape[1])).T


def to_row(tile):
    return jnp.sum(tile.T, axis=0, keepdims=True)


def kernel(
    total_rows, total_cents, n_dp, n_cent,
    emb_hbm, cent_hbm, out_w, out_m,
    emb, cent, energy, ch, zb, xg, xb, ucol, racc, co, cs, vb, vcol, rr, uz, wacc, wr, cacc, cfs, cfr,
    e_sem, t_sem, c_send, c_recv, v_send, v_recv, r_send, r_recv,
    z_send, z_recv, x_send, x_recv, y_send, y_recv, k_send, k_recv,
    u_send, u_recv, w_send, w_recv,
):
    n_z = n_dp // 2
    rows, width = emb.shape
    cents = cent.shape[0]
    block = cents // NB
    quarter = rows // n_cent
    part_rows = quarter // PIECES
    scale = 1.0 / (TAU * width)
    ratio = total_rows / total_cents
    d = lax.axis_index("dp")
    c = lax.axis_index("cent")
    z, x = d // 2, lax.rem(d, 2)
    y, core = c // 2, lax.rem(c, 2)
    dp_peers = [lax.rem(d + k, n_dp) for k in range(1, n_dp)]
    c_peers = [lax.rem(c + k, n_cent) for k in range(1, n_cent)]
    c_y = (1 - y) * 2 + core
    c_core = y * 2 + (1 - core)
    d_x = z * 2 + (1 - x)
    z_pair = z + 1 - 2 * lax.rem(z, 2)
    d_z = z_pair * 2 + x

    def block_at(t):
        pair = t // 2
        at_z = jnp.where(
            pair == 0, z, jnp.where(pair == 1, lax.rem(z + 2, n_z), jnp.where(pair == 2, 3 - z, z_pair))
        )
        return at_z * 2 + lax.rem(x + t + t // 6, 2)

    def remote(src, dst, ssem, rsem, dp, cn):
        return pltpu.make_async_remote_copy(
            src_ref=src, dst_ref=dst, send_sem=ssem, recv_sem=rsem,
            device_id={"dp": dp, "cent": cn}, device_id_type=MESH,
        )

    def cent_copy(b):
        at = pl.multiple_of(b * block, block)
        return pltpu.make_async_copy(
            cent_hbm.at[pl.ds(at, block)], cent.at[pl.ds(at, block)], t_sem.at[b]
        )

    emb_copy = pltpu.make_async_copy(emb_hbm, emb, e_sem)
    emb_copy.start()

    @pl.loop(0, NB)
    def _(t):
        cent_copy(block_at(t)).start()

    barrier = pltpu.get_barrier_semaphore()
    for peer in dp_peers:
        pl.semaphore_signal(barrier, inc=1, device_id={"dp": peer, "cent": c}, device_id_type=MESH)
    for peer in c_peers:
        pl.semaphore_signal(barrier, inc=1, device_id={"dp": d, "cent": peer}, device_id_type=MESH)

    emb_copy.wait()
    mine = pl.multiple_of(c * quarter, quarter)
    zb[z] = rms_rows(emb[pl.ds(mine, quarter), :]).astype(jnp.float32)
    pl.semaphore_wait(barrier, n_dp - 1 + n_cent - 1)

    low = z // 2
    first = z + 1 - 2 * low
    other = 2 * z - first
    last = 3 - 3 * low
    middle = (z == 1) | (z == 2)
    edge = jnp.logical_not(middle)
    near = jnp.where(middle, other, first)
    order = [near, last, 6 - z - near - last]
    n_items = 3 * PIECES

    def rows_of(p):
        return pl.ds(p * part_rows, part_rows)

    def z_copy(src, p, to, way, k):
        part = zb.at[src, rows_of(p)]
        return remote(part, part, z_send.at[way, k], z_recv.at[src, p], to * 2 + x, c)

    def z_arrival(i):
        j, p = divmod(i, PIECES)
        z_copy(order[j], p, first, 0, 0).wait_recv()

    def z_step(k):
        j, p = divmod(k, PIECES)
        if j == 0:

            @pl.when(edge)
            def _():
                z_copy(z, p, first, 0, k).start()

        @pl.when(middle)
        def _():
            if j == 1:
                z_arrival(k)
            z_copy(z if j == 0 else order[j], p, other, 1, k).start()
            if k < PIECES // 2:
                z_copy(z, p, first, 0, k).start()

    def z_between(i):
        if i < PIECES:

            @pl.when(middle)
            def _():
                z_copy(order[0], i, first, 0, PIECES + i).start()
        elif i < PIECES + PIECES // 2:
            p = i - PIECES // 2

            @pl.when(middle)
            def _():
                z_copy(z, p, first, 0, p).start()

    def z_drain():
        for p in range(PIECES):
            z_copy(z, p, first, 0, p).wait_send()

        @pl.when(middle)
        def _():
            for k in range(n_items):
                z_copy(z, k % PIECES, other, 1, k).wait_send()
            for p in range(PIECES):
                z_copy(z, p, first, 0, p + PIECES).wait_send()

    def x_copy(i):
        j, p = divmod(i, PIECES)
        return remote(
            zb.at[order[j], rows_of(p)], xg.at[order[j], c, rows_of(p)],
            x_send.at[i], x_recv.at[i], d_x, c,
        )

    def own_part(i, crossed):
        j, p = divmod(i, PIECES)
        return xg.at[order[j], c, rows_of(p)] if crossed else zb.at[order[j], rows_of(p)]

    def y_copy(i, crossed, who):
        j, p = divmod(i, PIECES)
        return remote(
            own_part(i, crossed), xg.at[order[j], who, rows_of(p)],
            y_send.at[i], y_recv.at[i], d, c_y,
        )

    def k_copy(i, crossed, who):
        j, p = divmod(i, PIECES)
        return remote(
            own_part(i, crossed), xg.at[order[j], who, rows_of(p)],
            k_send.at[i, 0], k_recv.at[i, 0], d, c_core,
        )

    def k_copy_y(i, who):
        j, p = divmod(i, PIECES)
        part = xg.at[order[j], who, rows_of(p)]
        return remote(part, part, k_send.at[i, 1], k_recv.at[i, 1], d, c_core)

    def spread(i, crossed):
        y_copy(i, crossed, c).start()
        k_copy(i, crossed, c).start()

    def crossing(j):
        return (None, edge, middle)[j], (None, middle, edge)[j]

    def stage_x(i):
        if i < PIECES:
            z_arrival(i)
            x_copy(i).start()
        else:

            @pl.when(crossing(i // PIECES)[0])
            def _():
                z_arrival(i)
                x_copy(i).start()

    def across(i):
        x_copy(i).wait()
        spread(i, True)

    def stage_y(i):
        if i < PIECES:
            across(i)
        else:

            @pl.when(edge)
            def _():
                across(i)

            @pl.when(middle)
            def _():
                spread(i, False)

    def stage_last(i):
        @pl.when(edge)
        def _():
            z_arrival(i)
            spread(i, False)

        @pl.when(middle)
        def _():
            across(i)

    def stage_core(i):
        y_copy(i, True, c_y).wait()
        k_copy_y(i, c_y).start()

    def stage_done(i):
        k_copy(i, True, c_core).wait()
        k_copy_y(i, c_core).wait()

    def step(plan):
        early = 2 * PIECES
        for k in plan[1]:
            if k < early:
                stage_x(k)
            elif k < n_items:
                stage_last(k)
            z_between(k)
            if early <= k + LAG_Y < n_items:
                stage_x(k + LAG_Y)
            if 0 <= k - LAG_Y < early:
                stage_y(k - LAG_Y)
            if 0 <= k - LAG_CORE < early:
                stage_core(k - LAG_CORE)
            if early <= k - LAG_Y < n_items:
                stage_core(k - LAG_Y)
        for k in plan[0]:
            z_step(k)

    def steps(where):
        step(PLAN[where])

    def steps_at(where, t):
        for at, plan in PLAN[where].items():

            @pl.when(t == at)
            def _():
                step(plan)

    def unpack(j):
        for p in range(PIECES):
            stage_done(j * PIECES + p)
        at = order[j] * rows
        for k in range(1, n_cent):
            who = lax.rem(c + k, n_cent)
            xb[pl.ds(pl.multiple_of(at + who * quarter, quarter), quarter), :] = xg[
                order[j], who
            ].astype(jnp.bfloat16)
        own = pl.ds(pl.multiple_of(at + c * quarter, quarter), quarter)
        if j == 0:
            xb[own, :] = xg[order[j], c].astype(jnp.bfloat16)
        else:
            crossed, straight = crossing(j)

            @pl.when(crossed)
            def _():
                xb[own, :] = xg[order[j], c].astype(jnp.bfloat16)

            @pl.when(straight)
            def _():
                xb[own, :] = zb[order[j]].astype(jnp.bfloat16)

    steps("start")
    base = pl.multiple_of(z * rows, rows)
    for i in range(n_cent):
        xb[pl.ds(base + i * quarter, quarter), :] = rms_rows(emb[i * quarter : (i + 1) * quarter, :])

    def c_copy(it, b, owner):
        return remote(co.at[it, b], cs.at[it, owner], c_send.at[it, b], c_recv.at[it, owner], b, c)

    def v_copy(it, owner, to):
        part = vb.at[it, owner]
        return remote(part, part, v_send.at[it, to], v_recv.at[it, owner], to, c)

    def r_copy(it, k, owner):
        part = rr.at[it, owner]
        return remote(part, part, r_send.at[it, k], r_recv.at[it, owner], d, c_peers[k])

    def column_part(it, t, b, col):
        row = jnp.sum(col, axis=0, keepdims=True)

        @pl.when(t == 0)
        def _():
            cs[it, d] = row

        @pl.when(t > 0)
        def _():
            co[it, b] = row
            c_copy(it, b, d).start()

    def exchange(it):
        rr[it, c] = to_row(racc[...])
        for k in range(n_cent - 1):
            r_copy(it, k, c).start()
        steps("sums%d" % it)
        for peer in dp_peers:
            c_copy(it, peer, peer).wait_recv()
        col_sum = cs[it, 0]
        for k in range(1, n_dp):
            col_sum = col_sum + cs[it, k]
        v_old = vb[it - 1, d] if it else jnp.ones((1, block), jnp.float32)
        vb[it, d] = jnp.sqrt(v_old * ratio / col_sum)
        if it < ITERS - 1:

            @pl.loop(1, NB)
            def _(t):
                v_copy(it, d, block_at(t)).start()
        else:
            v_copy(it, d, d_x).start()
            v_copy(it, d, d_z).start()
        steps("shared%d" % it)
        for k, peer in enumerate(c_peers):
            r_copy(it, k, peer).wait()
        row_sum = rr[it, 0]
        for k in range(1, n_cent):
            row_sum = row_sum + rr[it, k]
        u_old = uz[z] if it else jnp.ones((1, rows), jnp.float32)
        u_new = jnp.sqrt(u_old / row_sum)
        uz[z] = u_new
        if it < ITERS - 1:
            ucol[...] = to_column(u_new)

    wacc[...] = jnp.zeros_like(wacc)
    cacc[...] = jnp.zeros_like(cacc)
    racc[...] = jnp.zeros_like(racc)

    @pl.loop(0, NB)
    def _(t):
        steps_at("scores", t)
        b = block_at(t)
        at = pl.multiple_of(b * block, block)
        cent_copy(b).wait()
        ch_b = rms_rows(cent[pl.ds(at, block), :])
        ch[pl.ds(at, block), :] = ch_b
        col = jnp.zeros((8, block), jnp.float32)
        for i in range(n_cent):
            part = slice(i * quarter, (i + 1) * quarter)
            s = lax.dot_general(
                xb[pl.ds(base + i * quarter, quarter), :], ch_b, NT,
                preferred_element_type=jnp.float32,
            )
            e = jnp.exp(s * scale)
            energy[b, part, :] = e
            racc[part, :] += lane_tiles(e)
            col = col + jnp.sum(e.reshape(quarter // 8, 8, block), axis=0)
        column_part(0, t, b, col)

    exchange(0)

    group = 64
    for it in range(1, ITERS):
        racc[...] = jnp.zeros_like(racc)

        @pl.loop(0, NB)
        def _(t):
            steps_at("pass%d" % it, t)
            b = block_at(t)

            @pl.when(t > 0)
            def _():
                v_copy(it - 1, b, d_x).wait_recv()

            v_b = jnp.broadcast_to(vb[it - 1, b], (8, block))

            def rows_step(g, col):
                r0 = pl.multiple_of(g * group, group)
                for i in range(group // 8):
                    e = energy[b, pl.ds(r0 + i * 8, 8), :]
                    u8 = ucol[pl.ds(r0 + i * 8, 8), :]
                    col = col + e * jnp.concatenate([u8] * (block // 128), axis=1)
                    racc[pl.ds(r0 + i * 8, 8), :] += lane_tiles(e * v_b)
                return col

            col = lax.fori_loop(0, rows // group, rows_step, jnp.zeros((8, block), jnp.float32))
            column_part(it, t, b, col)

        exchange(it)

    def u_copy(k, owner):
        to = lax.rem(z + k, n_z)
        return remote(
            uz.at[owner], uz.at[owner], u_send.at[k - 1], u_recv.at[owner],
            to * 2 + lax.rem(x + k, 2), c,
        )

    for k in range(1, n_z):
        u_copy(k, z).start()
    final = ITERS - 1
    owners = (d_x, d_z, d, d)

    def column_scales(qs):
        for q in qs:
            s = q % 2
            vcol[q] = to_column(vb[final, owners[q]][:, s * CHUNK : (s + 1) * CHUNK])

    column_scales((2, 3))
    steps("u")

    def weigh(q, blocks, start=0, count=CHUNK):
        part = pl.ds(start, count)
        owner = jnp.where(q == 0, d_x, jnp.where(q == 1, d_z, d))
        at = pl.multiple_of(owner * block + lax.rem(q, 2) * CHUNK + start, count)
        cc = ch[pl.ds(at, count), :]
        v_tile = jnp.concatenate([vcol[q, part]] * (block // 128), axis=1)
        for first_row, u in blocks:
            xr = xb[pl.ds(pl.multiple_of(first_row, block), block), :]
            e = jnp.exp(lax.dot_general(cc, xr, NT, preferred_element_type=jnp.float32) * scale)
            cacc[q, part] += lane_tiles(e * u)
            w = ((total_cents * u) * e * v_tile).astype(jnp.bfloat16)
            wacc[q, part] += jnp.dot(w, xr, preferred_element_type=jnp.float32)

    def whole(src):
        return [
            (src * rows + h * block, uz[src][:, h * block : (h + 1) * block])
            for h in range(rows // block)
        ]

    n_out = 2 * (n_z - 1)

    def unit(t):
        late = jnp.maximum(t - n_out, 0)
        j = jnp.where(t < n_out, t, late) // 2
        src = jnp.where(j == 0, z, jnp.where(j == 1, order[0], jnp.where(j == 2, order[1], order[2])))
        weigh(lax.rem(t, 2) + jnp.where(t < n_out, 0, 2), whole(src))

    @pl.loop(0, n_out + AHEAD)
    def _(t):
        steps_at("weigh", t)

        @pl.when(t == 0)
        def _():
            v_copy(final, d_x, d_x).wait_recv()
            v_copy(final, d_z, d_z).wait_recv()
            column_scales((0, 1))

        @pl.when(t == 2)
        def _():
            unpack(0)
            for k in range(1, n_z):
                u_copy(k, lax.rem(z + k, n_z)).wait()

        @pl.when(t == 4)
        def _():
            unpack(1)

        unit(t)

    unpack(2)

    half = CHUNK // 2

    def w_copy(s, h):
        part = pl.ds(h * half, half)
        return remote(
            wacc.at[s, part], wr.at[s, part], w_send.at[2 * h + s], w_recv.at[2 * h + s],
            owners[s], c,
        )

    def f_copy(s):
        return remote(cfs.at[s], cfr.at[s], w_send.at[4 + s], w_recv.at[4 + s], owners[s], c)

    @pl.loop(0, 4)
    def _(t):
        weigh(lax.rem(t, 2), whole(order[2]), pl.multiple_of((t // 2) * half, half), half)
        for h in range(2):
            for s in range(2):

                @pl.when(t == 2 * h + s)
                def _():
                    w_copy(s, h).start()

    for s in range(2):
        cfs[s] = to_row(cacc[s])
        f_copy(s).start()

    @pl.loop(n_out + AHEAD, n_out + 2 * n_z)
    def _(t):
        unit(t)

    for q in (2, 3):
        cfs[q] = to_row(cacc[q])
    z_drain()
    for it in range(ITERS):

        @pl.loop(1, NB)
        def _(t):
            b = block_at(t)
            c_copy(it, b, d).wait_send()
            if it < final:
                v_copy(it, d, b).wait_send()

    v_copy(final, d, d_x).wait_send()
    v_copy(final, d, d_z).wait_send()
    for h in range(2):
        part = slice(h * half, (h + 1) * half)
        for s in range(2):
            w_copy(s, h).wait()
            w = wacc[2 + s, part] + wr[s, part]
            out_w[s, part] = w * lax.rsqrt(jnp.mean(w * w, axis=1, keepdims=True) + 1e-06)
    for s in range(2):
        f_copy(s).wait()
        lanes = slice(s * CHUNK, (s + 1) * CHUNK)
        out_m[:, lanes] = (
            vb[final, d][:, lanes] * (cfs[2 + s] + cfr[s]) * (total_cents / total_rows)
        )


def fused(embeddings, centroids):
    n_dp, n_cent = lax.axis_size("dp"), lax.axis_size("cent")
    rows, width = embeddings.shape
    cents = centroids.shape[0]
    n_z = n_dp // 2
    block = cents // NB
    quarter = rows // n_cent
    n_s = block // CHUNK
    n_items = 3 * PIECES
    f32 = jnp.float32
    dma = pltpu.SemaphoreType.DMA
    w, m = pl.pallas_call(
        functools.partial(
            kernel, float(rows * n_dp), float(cents * n_cent), n_dp, n_cent
        ),
        out_shape=(
            pltpu.VMEM((n_s, CHUNK, width), f32),
            pltpu.VMEM((1, block), f32),
        ),
        in_specs=[pl.BlockSpec(memory_space=pl.ANY)] * 2,
        out_specs=(pl.BlockSpec(memory_space=pltpu.VMEM),) * 2,
        scratch_shapes=[
            pltpu.VMEM((rows, width), jnp.bfloat16),
            pltpu.VMEM((cents, width), jnp.bfloat16),
            pltpu.VMEM((NB, rows, block), f32),
            pltpu.VMEM((cents, width), jnp.bfloat16),
            pltpu.VMEM((n_z, quarter, width), f32),
            pltpu.VMEM((n_z, n_cent, quarter, width), f32),
            pltpu.VMEM((n_z * rows, width), jnp.bfloat16),
            pltpu.VMEM((rows, 128), f32),
            pltpu.VMEM((rows, 128), f32),
            pltpu.VMEM((ITERS, NB, 1, block), f32),
            pltpu.VMEM((ITERS, n_dp, 1, block), f32),
            pltpu.VMEM((ITERS, n_dp, 1, block), f32),
            pltpu.VMEM((2 * n_s, CHUNK, 128), f32),
            pltpu.VMEM((ITERS, n_cent, 1, rows), f32),
            pltpu.VMEM((n_z, 1, rows), f32),
            pltpu.VMEM((2 * n_s, CHUNK, width), f32),
            pltpu.VMEM((n_s, CHUNK, width), f32),
            pltpu.VMEM((2 * n_s, CHUNK, 128), f32),
            pltpu.VMEM((2 * n_s, 1, CHUNK), f32),
            pltpu.VMEM((n_s, 1, CHUNK), f32),
            dma,
            dma((NB,)),
            dma((ITERS, n_dp)),
            dma((ITERS, n_dp)),
            dma((ITERS, n_dp)),
            dma((ITERS, n_dp)),
            dma((ITERS, n_cent - 1)),
            dma((ITERS, n_cent)),
            dma((2, n_items)),
            dma((n_z, PIECES)),
            dma((n_items,)),
            dma((n_items,)),
            dma((n_items,)),
            dma((n_items,)),
            dma((n_items, 2)),
            dma((n_items, 2)),
            dma((n_z - 1,)),
            dma((n_z,)),
            dma((3 * n_s,)),
            dma((3 * n_s,)),
        ],
        compiler_params=pltpu.CompilerParams(
            collective_id=0, has_side_effects=True, vmem_limit_bytes=60 * 2**20
        ),
    )(embeddings, centroids)
    return w.reshape(block, width), m.reshape(block)


def column_total(weights, energy):
    return lax.psum(jnp.dot(weights, energy, precision=lax.Precision.HIGHEST), "dp")


def local(embeddings, centroids):
    n_data = lax.axis_size("dp")
    xh = rms_rows(embeddings)
    ch = rms_rows(centroids)
    local_rows, width = xh.shape
    local_cents = ch.shape[0]
    total_rows = float(local_rows * n_data)
    total_cents = float(local_cents * lax.axis_size("cent"))
    scores = lax.dot_general(xh, ch, NT, preferred_element_type=jnp.float32)
    energy = jnp.exp(scores * (1.0 / (TAU * width)))
    u = jnp.ones((local_rows,), jnp.float32)
    v = jnp.ones((local_cents,), jnp.float32)
    for step_index in range(ITERS):
        rows_sum = lax.psum(jnp.dot(energy, v, precision=lax.Precision.HIGHEST), "cent")
        cols = column_total(u, energy)
        u, v = (jnp.sqrt(u / rows_sum), jnp.sqrt(v * (total_rows / total_cents) / cols))
    cols = column_total(u, energy)
    plan = (total_cents * u[:, None] * energy * v[None, :]).astype(jnp.bfloat16)
    share = local_cents // n_data
    weighted = lax.dot_general(
        plan, xh, (((0,), (0,)), ((), ())), preferred_element_type=jnp.float32
    )
    mine = lax.psum_scatter(weighted, "dp", scatter_dimension=0, tiled=True)
    mass_all = v * cols * (total_cents / total_rows)
    column_mass = lax.dynamic_slice_in_dim(mass_all, lax.axis_index("dp") * share, share, 0)
    new_centroids = mine * lax.rsqrt(jnp.mean(mine * mine, axis=1, keepdims=True) + 1e-06)
    return (new_centroids, column_mass)


def solution(mesh):
    in_specs = (P("dp", None), P("cent", None))
    out_specs = (P(("cent", "dp"), None), P(("cent", "dp")))
    small = mesh.shape["dp"] == NB and mesh.shape["cent"] == 4
    body = fused if small else local
    return jax.shard_map(body, mesh=mesh, in_specs=in_specs, out_specs=out_specs, check_vma=False)
```
